128 devices in a mesh: mem: 16 (over z, y), dp: 8 (over x, core).
Axes of the slice: x: 4, y: 4, z: 4, core: 2. Of those that a mesh axis runs over, the one named last changes fastest.
Arguments:
- grad_out: bfloat16 [65536, 4096], P(('mem', 'dp')), may hold values from -6 to 6
- scores: float32 [65536, 2], P(('mem', 'dp')), may hold values from -4 to 4
- row_ids: int32 [65536, 2], P(('mem', 'dp')), may hold values from 0 to 16383, as said below
- proj_ids: int32 [65536, 2], P(('mem', 'dp')), may hold values from 0 to 1
- values: bfloat16 [16384, 1024], P('mem'), may hold values from -0.1875 to 0.1875
- proj_w: bfloat16 [2, 1024, 4096], P(None, None, 'mem'), may hold values from -0.09375 to 0.09375
Outputs:
- score_grads: float32 [65536, 2], P(('mem', 'dp'))
- value_grads: bfloat16 [16384, 1024], P(('mem', 'dp'))
- proj_grads: float32 [2, 1024, 4096], P(None, 'dp', 'mem')
The draws below stay inside these ranges and needn't reach their ends.
Inputs may be any that keep to these rules, and one draw needn't show every extreme that they name: `row_ids`: row 1024 * o + r lies on index o along mem. Of the 1024 selections of one device at most 128 name rows of one index along mem; among the devices that share one index along dp, one index along mem receives exactly 128 selections from every one of them.
All inputs are finite; a program needn't handle non-finite values.
Results may differ from the reference program's by a relative error of at most 0.012.
Values may be sent and summed in bfloat16 or wider, within the bound.
A program may use at most 128 MiB of HBM per device.

```python
import jax
import jax.numpy as jnp
from jax import lax

D = 4096
VW = 1024
NPROJ = 2
SEL = 2
TOK_DEV = 512
ROWS_DEV = 1024
TOKENS = 65536
ROWS = 16384
N_MEM = 16
N_DP = 8


def draw_row_ids(key, part):
    blocks = N_MEM * N_DP
    sel_count = TOK_DEV * SEL
    capacity = 2 * sel_count // N_MEM
    others = N_MEM - 1
    hot_owner = jax.random.randint(jax.random.fold_in(key, 11), (N_DP,), 0, N_MEM)

    def one_block(block):
        block_key = jax.random.fold_in(jax.random.fold_in(key, 23), block)
        key_order, key_bits, key_slots, key_rows = jax.random.split(block_key, 4)
        hot = hot_owner[block % N_DP]
        owner_range = jnp.arange(N_MEM, dtype=jnp.int32)
        ranking = jax.random.randint(key_order, (N_MEM,), 0, 1 << 20) * N_MEM + owner_range
        ranking = jnp.where(owner_range == hot, -1, ranking)
        order = jnp.argsort(ranking, stable=True).astype(jnp.int32)
        position = jnp.arange(sel_count, dtype=jnp.int32)
        later = jnp.maximum(position - capacity, 0)
        klass = later % others
        shift_bit = jax.random.randint(key_bits, (sel_count,), 0, 2)
        other_owner = order[1 + (klass + shift_bit) % others]
        owner = jnp.where(position < capacity, hot, other_owner)
        shuffle = jax.random.permutation(key_slots, sel_count)
        owner = owner[shuffle]
        local_row = jax.random.randint(key_rows, (sel_count,), 0, ROWS_DEV)
        return (owner * ROWS_DEV + local_row).astype(jnp.int32)
    every = jax.vmap(one_block)(jnp.arange(blocks, dtype=jnp.int32))
    return every.reshape(blocks * TOK_DEV, SEL)


def plant(result, rng, low, top_value):
    place = [jax.random.randint(jax.random.fold_in(rng, axis), (), 0, length) for axis, length in enumerate(result.shape)]
    widest = result.shape.index(max(result.shape))
    beside = place[:widest] + [(place[widest] + 1) % result.shape[widest]] + place[widest + 1:]
    return result.at[tuple(place)].set(low).at[tuple(beside)].set(top_value)


def block_levels(rng, dims, cuts, smallest, high):
    level, own = 1.0, jax.random.fold_in(rng, 6)
    for axis_at, blocks in cuts:
        draws = jnp.exp(jax.random.uniform(jax.random.fold_in(own, axis_at), (blocks,), jnp.float32, smallest / len(cuts), high / len(cuts)))
        level = level * jnp.repeat(draws, dims[axis_at] // blocks).reshape([-1 if axis == axis_at else 1 for axis in range(len(dims))])
    return level


def bell_draw(rng, extent, deviation, reach, cuts=(), held_as=jnp.bfloat16):
    values = deviation * jax.random.normal(rng, extent, jnp.float32)
    if cuts:
        values = values * block_levels(rng, extent, cuts, -0.22, 0.18)
    return jnp.clip(values, -reach, reach).astype(held_as)


def setup_inputs(seed: int = 0) -> dict:
    streams_of = jax.random.split(jax.random.key(seed), 7)
    grad_out = bell_draw(streams_of[0], (TOKENS, D), 1.0, 6.0, ((0, 128),))
    scores = bell_draw(streams_of[1], (TOKENS, SEL), 1.0, 4.0, ((0, 128),), jnp.float32)
    row_ids = draw_row_ids(jax.random.fold_in(streams_of[6], 71), 0)
    proj_ids = plant(jax.random.randint(streams_of[3], (TOKENS, SEL), 0, NPROJ), jax.random.fold_in(streams_of[3], 1), 0, NPROJ - 1).astype(jnp.int32)
    values = bell_draw(streams_of[4], (ROWS, VW), VW ** -0.5, 0.1875, ((0, 16),))
    proj_w = bell_draw(streams_of[5], (NPROJ, VW, D), D ** -0.5, 0.09375, ((2, 16),))
    return {"grad_out": grad_out, "scores": scores, "row_ids": row_ids, "proj_ids": proj_ids, "values": values, "proj_w": proj_w}


def reference(grad_out, scores, row_ids, proj_ids, values, proj_w):
    token_total = grad_out.shape[0]
    picked = jnp.zeros((token_total, SEL, VW), jnp.float32)
    for which in range(NPROJ):
        projected = jnp.dot(grad_out, proj_w[which].T, preferred_element_type=jnp.float32)
        picked = picked + jnp.where((proj_ids == which)[:, :, None], projected[:, None, :], 0.0)
    contrib = (scores[:, :, None] * picked).astype(jnp.bfloat16)
    flat_rows = row_ids.reshape(-1)
    value_grads = jnp.zeros((ROWS, VW), jnp.float32).at[flat_rows].add(contrib.reshape(-1, VW).astype(jnp.float32))
    value_grads = value_grads.astype(jnp.bfloat16)
    chosen = jnp.take(values, flat_rows, axis=0).reshape(token_total, SEL, VW)
    chosen_wide = chosen.astype(jnp.float32)
    score_grads = jnp.sum(picked * chosen_wide, axis=2)
    mix_list = []
    for which in range(NPROJ):
        weight = jnp.where(proj_ids == which, scores, 0.0)
        mix_list.append(jnp.sum(weight[:, :, None] * chosen_wide, axis=1).astype(jnp.bfloat16))
    mixes = jnp.stack(mix_list, axis=0)
    blocks = N_MEM * N_DP
    mix_blocks = mixes.reshape(NPROJ, blocks, TOK_DEV, VW).transpose(1, 0, 2, 3)
    grad_blocks = grad_out.reshape(blocks, TOK_DEV, D)

    def add_block(carry, pair):
        mix_block, grad_block = pair
        term = jnp.einsum('ptv,td->pvd', mix_block.astype(jnp.float32), grad_block.astype(jnp.float32))
        term = lax.optimization_barrier(term.astype(jnp.bfloat16))
        return carry + term.astype(jnp.float32), None

    proj_grads, unused = lax.scan(add_block, jnp.zeros((NPROJ, VW, D), jnp.float32), (mix_blocks, grad_blocks))
    return score_grads, value_grads, proj_grads
```

```python
import jax
import jax.numpy as jnp
from jax import lax
from jax.experimental import pallas as pl
from jax.experimental.pallas import tpu as pltpu
from jax.sharding import PartitionSpec as P

F32 = jnp.float32
BF16 = jnp.bfloat16
I32 = jnp.int32
MESH = pl.DeviceIdType.MESH
ORDER = (4, 1, 12, 3, 8, 2, 5, 15, 7, 13, 9, 6, 11, 14, 10)
PACKS = tuple(sum(label * 16**place for place, label in enumerate(ORDER[at : at + 5])) for at in (0, 5, 10))


def in_order(body):
    for pack in PACKS:

        def step(_, carry):
            body(carry % 16)
            return carry // 16

        lax.fori_loop(0, 5, step, jnp.int32(pack))


def loop(count, body, start=0):
    def step(index, carry):
        body(index)
        return carry

    lax.fori_loop(start, count, step, jnp.int32(0))


def nn(a, b):
    return lax.dot_general(a, b, (((1,), (0,)), ((), ())), preferred_element_type=F32)


def nt(a, b):
    return lax.dot_general(a, b, (((1,), (1,)), ((), ())), preferred_element_type=F32)


def hot(condition):
    return jnp.where(condition, F32(1), F32(0)).astype(BF16)


def kernel(
    grad_hbm, scores_ref, rows_ref, proj_ref, values_hbm, w_hbm,
    sg_out, vg_out, pg_out,
    gbuf, wg, vh, outbox, chosen_in, contrib_in, chosen, pb, ra, rb, rl, rr, fr,
    vgs, vgr, vgp_s, vgp_r, metas, slotr, slotc, reqs, reqr, sgs, sgr,
    lsem, core_s, core_r, req_s, req_r, val_s, val_r, wq_s, wq_r, w1_s, w1_r, w2_s, w2_r, wx_s, wx_r,
    p2_s, p2_r, p1_s, p1_r, p3_s, p3_r, con_s, con_r, fin_s, fin_r, vx_s, vx_r,
):
    m = lax.axis_index("mem")
    d = lax.axis_index("dp")
    z, y = m // 4, m % 4
    x, c = d // 2, d % 2
    partner = (m, x * 2 + (1 - c))

    def peer_mem(label):
        return ((z + label // 4) % 4) * 4 + (y + label % 4) % 4

    def peer(label):
        return (peer_mem(label), d)

    def xpeer(step):
        return (m, ((x + step) % 4) * 2 + c)

    def remote(src, dst, send, recv, device):
        return pltpu.make_async_remote_copy(
            src_ref=src, dst_ref=dst, send_sem=send, recv_sem=recv, device_id=device, device_id_type=MESH
        )

    local_copies = [pltpu.make_async_copy(grad_hbm, gbuf.at[0], lsem.at[0])]
    for j in range(4):
        block = (x + j) % 4
        local_copies.append(
            pltpu.make_async_copy(
                values_hbm.at[:, pl.ds(pl.multiple_of(block * 256 + c * 128, 128), 128)],
                vh.at[:, pl.ds(j * 128, 128)],
                lsem.at[1 + j],
            )
        )
    w_copies = []
    for p in range(2):
        for j in range(4):
            w_copies.append(
                pltpu.make_async_copy(
                    w_hbm.at[p, (x + j) % 4, c], wg.at[0, p, pl.ds(j * 128, 128)], lsem.at[5 + p * 4 + j]
                )
            )
    for copy in w_copies + local_copies:
        copy.start()

    barrier = pltpu.get_barrier_semaphore()
    for label in range(1, 16):
        pl.semaphore_signal(barrier, inc=1, device_id=peer(label), device_id_type=MESH)
    for step in range(1, 4):
        pl.semaphore_signal(barrier, inc=1, device_id=xpeer(step), device_id_type=MESH)
    pl.semaphore_signal(barrier, inc=1, device_id=partner, device_id_type=MESH)

    lane = lax.broadcasted_iota(I32, (512, 128), 1)
    meta = jnp.zeros((512, 128), F32)
    for at, ref in enumerate((rows_ref, proj_ref, scores_ref)):
        for s in range(2):
            meta = jnp.where(lane == 2 * at + s, ref[:, s : s + 1].astype(F32), meta)
    metas[0] = meta
    pl.semaphore_wait(barrier, 19)

    meta_copy = remote(metas.at[0], metas.at[1], core_s.at[0], core_r.at[0], partner)
    meta_copy.start()
    for copy in w_copies:
        copy.wait()

    def quarter(label):
        here = wg.at[0, 1, pl.ds(0, 128)]
        return remote(here, wg.at[label, 1, pl.ds(0, 128)], wq_s.at[label], wq_r.at[label], peer(label))

    def stage_one(half, step):
        label = step * 4 if half == 0 else step
        rows = pl.ds(half * 256, 256)
        return remote(
            wg.at[0, 0, rows], wg.at[label, 0, rows], w1_s.at[half, step], w1_r.at[half, step], peer(label)
        )

    def stage_two(half, held, step):
        source, move = (held * 4, step) if half == 0 else (held, step * 4)
        rows = pl.ds(half * 256, 256)
        return remote(
            wg.at[source, 0, rows],
            wg.at[source + move, 0, rows],
            w2_s.at[half, source + move],
            w2_r.at[half, source + move],
            peer(move),
        )

    def along_x(label, step):
        return remote(
            wg.at[label, 1, pl.ds(0, 128)],
            wg.at[label, 1, pl.ds((4 - step) * 128, 128)],
            wx_s.at[label, step],
            wx_r.at[label, 4 - step],
            xpeer(step),
        )

    in_order(lambda label: quarter(label).start())
    for step in (1, 3, 2):
        for half in range(2):
            stage_one(half, step).start()
    grad_copy = remote(grad_hbm, gbuf.at[1], core_s.at[1], core_r.at[1], partner)
    grad_copy.start()

    reqs[...] = jnp.zeros_like(reqs)
    for k in range(2):
        if k == 1:
            meta_copy.wait_recv()
        flat = jnp.transpose(metas[k])
        row = jnp.concatenate([flat[0:1, :], flat[1:2, :]], axis=1).astype(I32)
        owner = row >> 10
        label = ((((owner >> 2) - z) & 3) << 2) | (((owner & 3) - y) & 3)
        hit = label == lax.broadcasted_iota(I32, (16, 1024), 0)
        hits = hot(hit)
        before = []
        for part in range(4):
            upper = lax.broadcasted_iota(I32, (1024, 256), 0) < lax.broadcasted_iota(I32, (1024, 256), 1) + part * 256
            before.append(nn(hits, hot(upper)))
        before = jnp.concatenate(before, axis=1)
        rank = jnp.sum(jnp.where(hit, before, F32(0)), axis=0, keepdims=True)
        slot = label.astype(F32) * 128 + rank
        slotr[k] = jnp.broadcast_to(slot, (8, 1024)).astype(I32)
        slotc[k] = jnp.transpose(jnp.broadcast_to(slot, (128, 1024)))
        rank_column = jnp.transpose(jnp.broadcast_to(rank, (128, 1024)))
        places = hot(rank_column == lax.broadcasted_iota(I32, (1024, 128), 1).astype(F32))
        number = (row & 1023) + 1
        upper_digit = jnp.where(hit, (number >> 5).astype(F32), F32(0)).astype(BF16)
        lower_digit = jnp.where(hit, (number & 31).astype(F32), F32(0)).astype(BF16)
        asked = nn(upper_digit, places) * 32 + nn(lower_digit, places) - 1
        for label_at in range(16):
            reqs[label_at, k : k + 1, :] = asked[label_at : label_at + 1, :]

    def request(label):
        return remote(reqs.at[label], reqr.at[label], req_s.at[label], req_r.at[label], peer(label))

    in_order(lambda label: request(label).start())
    reqr[0] = reqs[0]
    for copy in local_copies:
        copy.wait()

    def value_copy(label):
        back = ((z + 4 - label // 4) % 4) * 4 + (y + 4 - label % 4) % 4
        return remote(
            outbox.at[:, label], chosen_in.at[:, label], val_s.at[label], val_r.at[label], (back, d)
        )

    def look_up(label, target):
        parts = []
        for k in range(2):
            column = jnp.transpose(jnp.broadcast_to(reqr[label, k : k + 1, :], (128, 128)))
            base = lax.broadcasted_iota(I32, (128, 128), 1).astype(F32)
            parts.append(jnp.concatenate([hot(column == base + 128 * part) for part in range(8)], axis=1))
        found = nn(jnp.concatenate(parts, axis=0), vh[...]).astype(BF16)
        target[0, label] = found[:128]
        target[1, label] = found[128:]

    def serve(label):
        request(label).wait_recv()
        look_up(label, outbox)
        value_copy(label).start()

    in_order(serve)
    look_up(0, chosen_in)

    for held in range(4):
        if held:
            for half in range(2):
                stage_one(half, held).wait_recv()
        for step in (1, 3, 2):
            for half in range(2):
                stage_two(half, held, step).start()

    def forward(label):
        quarter(label).wait_recv()
        for step in (1, 3, 2):
            along_x(label, step).start()

    in_order(forward)

    in_order(lambda label: value_copy(label).wait_recv())
    grad_copy.wait_recv()

    def choose(at):
        k, tile = at // 2, at % 2
        column = slotc[k, pl.ds(pl.multiple_of(tile * 512, 512), 512), :]
        base = lax.broadcasted_iota(I32, (512, 128), 1).astype(F32)
        table = jnp.concatenate([hot(column == base + 128 * part) for part in range(16)], axis=1)
        rows = nn(table, chosen_in[k].reshape(2048, 512))
        chosen[k, pl.ds(pl.multiple_of(tile * 512, 512), 512), :] = rows.astype(BF16)

    loop(4, choose)

    def scope_mix(mt):
        for k in range(2):

            def mix(tile):
                here = pl.ds(pl.multiple_of(tile * 128, 128), 128)
                first = chosen[k, here, :].astype(F32)
                second = chosen[k, pl.ds(pl.multiple_of(512 + tile * 128, 128), 128), :].astype(F32)
                for p in range(2):
                    w0 = jnp.where(metas[k, here, 2:3] == p, metas[k, here, 4:5], F32(0))
                    w1 = jnp.where(metas[k, here, 3:4] == p, metas[k, here, 5:6], F32(0))
                    turned = jnp.transpose(w0 * first + w1 * second).astype(BF16)
                    for j in range(4):
                        mt[
                            pl.ds(j * 256 + p * 128, 128),
                            pl.ds(pl.multiple_of(k * 512 + tile * 128, 128), 128),
                        ] = turned[j * 128 : (j + 1) * 128]

            loop(4, mix)

        for a in range(4):

            def partial(b):
                columns = pl.ds(pl.multiple_of((((z + a) % 4) * 4 + (y + b) % 4) * 256, 256), 256)
                term = nn(mt[:, :512], gbuf[0, :, columns]) + nn(mt[:, 512:], gbuf[1, :, columns])
                term = term.astype(BF16)
                for j in range(4):
                    pb[j, a * 4 + b] = term[j * 256 : (j + 1) * 256]

            loop(4, partial)
            two_away(a).start()
            if a < 2:
                to_left(a).start()
            else:
                to_right(a).start()

    def span(a):
        return pl.ds(a * 4, 4)

    def two_away(a):
        if a < 2:
            return remote(pb.at[2, span(a)], ra.at[span(a)], p2_s.at[a], p2_r.at[a], xpeer(1))
        return remote(pb.at[2, span(a)], rb.at[span(a - 2)], p2_s.at[a], p2_r.at[a], xpeer(3))

    def to_right(a):
        return remote(pb.at[1, span(a)], rl.at[span(a)], p1_s.at[a], p1_r.at[a], xpeer(1))

    def to_left(a):
        return remote(pb.at[3, span(a)], rr.at[span(a)], p3_s.at[a], p3_r.at[a], xpeer(3))

    pl.run_scoped(scope_mix, pltpu.VMEM((1024, 1024), BF16))

    def merge(a):
        two_away(a).wait_recv()
        block, arrived, shift = (1, ra, 0) if a < 2 else (3, rb, 8)

        def add(b):
            at = a * 4 + b
            pb[block, at] = (pb[block, at].astype(F32) + arrived[at - shift].astype(F32)).astype(BF16)

        loop(4, add)
        (to_right(a) if a < 2 else to_left(a)).start()

    def contrib_copy(label):
        return remote(outbox.at[:, label], contrib_in.at[:, label], con_s.at[label], con_r.at[label], peer(label))

    def score_copy():
        return remote(sgs.at[1], sgr, core_s.at[2], core_r.at[2], partner)

    def scope_pick(pr, contrib):
        def columns_of(label):
            return pl.ds(pl.multiple_of(peer_from(label) * 256, 256), 256)

        def peer_from(label):
            return ((z + 4 - label // 4) % 4) * 4 + (y + 4 - label % 4) % 4

        def project(label, p, first=False):
            for k in range(2):
                term = nt(gbuf[k, :, columns_of(label)], wg[label, p])
                here = (pl.ds(k * 512, 512), pl.ds(p * 512, 512))
                pr[here] = term if first else pr[here] + term

        for p in (1, 0):
            project(0, p, True)

        def second(label):
            for step in range(1, 4):
                along_x(label, 4 - step).wait_recv()
            project(label, 1)

        loop(16, second, 1)
        merge(0)
        merge(2)
        for held in range(1, 4):
            for half in range(2):
                stage_two(half, 0, held).wait_recv()

        def from_stage(held):
            for half in range(2):
                for step in range(1, 4):
                    stage_two(half, held, step).wait_recv()

        for held in range(1, 4):
            from_stage(held)
        loop(16, lambda label: project(label, 0), 1)
        merge(1)
        merge(3)

        in_order(lambda label: value_copy(label).wait_send())
        for k in range(2):

            def pick(tile):
                here = pl.ds(pl.multiple_of(tile * 128, 128), 128)
                wide = pr[pl.ds(pl.multiple_of(k * 512 + tile * 128, 128), 128), :]
                lanes = lax.broadcasted_iota(I32, (128, 128), 1)
                kept = jnp.zeros((128, 128), F32)
                for s in range(2):
                    rows = pl.ds(pl.multiple_of(s * 512 + tile * 128, 128), 128)
                    picked = jnp.where(metas[k, here, 2 + s : 3 + s] == 0, wide[:, :512], wide[:, 512:])
                    contrib[k, rows, :] = (metas[k, here, 4 + s : 5 + s] * picked).astype(BF16)
                    total = jnp.sum(picked * chosen[k, rows, :].astype(F32), axis=1, keepdims=True)
                    kept = jnp.where(lanes == s, total, kept)
                sgs[k, here, :] = kept

            loop(4, pick)
        score_copy().start()

        def pack(label, target):
            for k in range(2):
                places = lax.broadcasted_iota(I32, (128, 1024), 0) + label * 128
                target[k, label] = nn(hot(slotr[k, 0:1, :] == places), contrib[k]).astype(BF16)

        def send(label):
            pack(label, outbox)
            contrib_copy(label).start()

        in_order(send)
        pack(0, contrib_in)

    pl.run_scoped(scope_pick, pltpu.VMEM((1024, 1024), F32), pltpu.VMEM((2, 1024, 512), BF16))

    def final_copy(label):
        return remote(pb.at[0, label], fr.at[label], fin_s.at[label], fin_r.at[label], peer(label))

    for a in (2, 0, 3, 1):
        to_right(a).wait_recv()
        to_left(a).wait_recv()

        def finish(b):
            at = a * 4 + b
            total = pb[0, at].astype(F32) + rl[at].astype(F32) + rr[at].astype(F32)
            pb[0, at] = total.astype(BF16)

        loop(4, finish)
        for b in range(4):
            if a * 4 + b:
                final_copy(a * 4 + b).start()

    def vg_copy(step):
        return remote(vgs.at[step], vgr.at[step], vx_s.at[step], vx_r.at[step], xpeer(step))

    def vg_partner():
        return remote(vgp_s, vgp_r, core_s.at[3], core_r.at[3], partner)

    def scope_values(vg):
        def gather(label, first=False):
            parts = []
            for k in range(2):
                places = lax.broadcasted_iota(I32, (1024, 128), 0).astype(F32)
                parts.append(hot(places == reqr[label, k : k + 1, :]))
            rows = jnp.concatenate([contrib_in[0, label], contrib_in[1, label]], axis=0)
            term = nn(jnp.concatenate(parts, axis=1), rows)
            vg[...] = term if first else vg[...] + term

        gather(0, True)

        def arrive(label):
            contrib_copy(label).wait_recv()
            gather(label)

        in_order(arrive)
        for step in (1, 3, 2):
            rows = pl.ds(pl.multiple_of(((x + step) % 4) * 256, 256), 256)
            for j in range(4):
                vgs[step, :, pl.ds(j * 128, 128)] = vg[rows, pl.ds((step + j) % 4 * 128, 128)].astype(BF16)
            vg_copy(step).start()
        own = vg[pl.ds(pl.multiple_of(x * 256, 256), 256), :]
        for step in (1, 3, 2):
            vg_copy(step).wait_recv()
            own = own + vgr[step].astype(F32)
        vg[:256, :] = own
        vgp_s[...] = vg[pl.ds(pl.multiple_of((1 - c) * 128, 128), 128), :].astype(BF16)
        vg_partner().start()
        mine = vg[pl.ds(pl.multiple_of(c * 128, 128), 128), :].astype(BF16)
        for j in range(4):
            at = pl.multiple_of(((x + j) % 4) * 256 + c * 128, 128)
            vg_out[:, pl.ds(at, 128)] = mine[:, j * 128 : (j + 1) * 128]

    pl.run_scoped(scope_values, pltpu.VMEM((1024, 512), F32))

    in_order(lambda label: final_copy(label).wait_recv())
    for p in range(2):
        rows = pl.ds(p * 128, 128)
        total = pb[0, 0, rows, :].astype(F32)
        for label in range(1, 16):
            total = total + fr[label, rows, :].astype(F32)
        pg_out[p] = total

    score_copy().wait_recv()
    sg_out[...] = sgs[0, :, 0:2] + sgr[:, 0:2]

    vg_partner().wait_recv()
    other = vgp_r[...]
    for j in range(4):
        at = pl.multiple_of(((x + j) % 4) * 256 + (1 - c) * 128, 128)
        vg_out[:, pl.ds(at, 128)] = other[:, j * 128 : (j + 1) * 128]

    meta_copy.wait_send()
    grad_copy.wait_send()
    score_copy().wait_send()
    vg_partner().wait_send()

    def sent(label):
        quarter(label).wait_send()
        request(label).wait_send()
        contrib_copy(label).wait_send()
        final_copy(label).wait_send()
        for step in range(1, 4):
            along_x(label, step).wait_send()

    loop(16, sent, 1)
    for step in range(1, 4):
        vg_copy(step).wait_send()
        for half in range(2):
            stage_one(half, step).wait_send()
            for held in range(4):
                stage_two(half, held, step).wait_send()
    for a in range(4):
        two_away(a).wait_send()
        to_right(a).wait_send()
        to_left(a).wait_send()


def local(grad_out, scores, row_ids, proj_ids, values, proj_w):
    vmem = pl.BlockSpec(memory_space=pltpu.VMEM)
    anywhere = pl.BlockSpec(memory_space=pl.ANY)
    dma = pltpu.SemaphoreType.DMA
    return pl.pallas_call(
        kernel,
        out_shape=(
            jax.ShapeDtypeStruct((512, 2), F32),
            jax.ShapeDtypeStruct((128, 1024), BF16),
            jax.ShapeDtypeStruct((2, 128, 256), F32),
        ),
        in_specs=[anywhere, vmem, vmem, vmem, anywhere, anywhere],
        out_specs=(vmem, vmem, vmem),
        scratch_shapes=[
            pltpu.VMEM((2, 512, 4096), BF16),
            pltpu.VMEM((16, 2, 512, 256), BF16),
            pltpu.VMEM((1024, 512), BF16),
            pltpu.VMEM((2, 16, 128, 512), BF16),
            pltpu.VMEM((2, 16, 128, 512), BF16),
            pltpu.VMEM((2, 16, 128, 512), BF16),
            pltpu.VMEM((2, 1024, 512), BF16),
            pltpu.VMEM((4, 16, 256, 256), BF16),
            pltpu.VMEM((8, 256, 256), BF16),
            pltpu.VMEM((8, 256, 256), BF16),
            pltpu.VMEM((16, 256, 256), BF16),
            pltpu.VMEM((16, 256, 256), BF16),
            pltpu.VMEM((16, 256, 256), BF16),
            pltpu.VMEM((4, 256, 512), BF16),
            pltpu.VMEM((4, 256, 512), BF16),
            pltpu.VMEM((128, 512), BF16),
            pltpu.VMEM((128, 512), BF16),
            pltpu.VMEM((2, 512, 128), F32),
            pltpu.VMEM((2, 8, 1024), I32),
            pltpu.VMEM((2, 1024, 128), F32),
            pltpu.VMEM((16, 8, 128), F32),
            pltpu.VMEM((16, 8, 128), F32),
            pltpu.VMEM((2, 512, 128), F32),
            pltpu.VMEM((512, 128), F32),
            dma((13,)),
            dma((4,)),
            dma((4,)),
            dma((16,)),
            dma((16,)),
            dma((16,)),
            dma((16,)),
            dma((16,)),
            dma((16,)),
            dma((2, 4)),
            dma((2, 4)),
            dma((2, 16)),
            dma((2, 16)),
            dma((16, 4)),
            dma((16, 4)),
            dma((4,)),
            dma((4,)),
            dma((4,)),
            dma((4,)),
            dma((4,)),
            dma((4,)),
            dma((16,)),
            dma((16,)),
            dma((16,)),
            dma((16,)),
            dma((4,)),
            dma((4,)),
        ],
        compiler_params=pltpu.CompilerParams(
            collective_id=0, has_side_effects=True, vmem_limit_bytes=67043328
        ),
        name="step",
    )(grad_out, scores, row_ids, proj_ids, values, proj_w.reshape(2, 4, 2, 128, 256))


def solution(mesh):
    return jax.shard_map(
        local,
        mesh=mesh,
        in_specs=(
            P(("mem", "dp"), None),
            P(("mem", "dp"), None),
            P(("mem", "dp"), None),
            P(("mem", "dp"), None),
            P("mem", None),
            P(None, None, "mem"),
        ),
        out_specs=(P(("mem", "dp"), None), P(("mem", "dp"), None), P(None, "dp", "mem")),
        check_vma=False,
    )
```

```python
import jax
import jax.numpy as jnp
from jax import lax
from jax.experimental import pallas as pl
from jax.experimental.pallas import tpu as pltpu
from jax.sharding import PartitionSpec as P

F32 = jnp.float32
BF16 = jnp.bfloat16
I32 = jnp.int32
MESH = pl.DeviceIdType.MESH
ORDER = (4, 1, 12, 3, 8, 2, 5, 15, 7, 13, 9, 6, 11, 14, 10)
JORDER = (2, 3, 1, 0)
PLACE = (3, 2, 0, 1)
WROW = (0, 2, 1, 3)
PACKS = tuple(sum(label * 16**place for place, label in enumerate(ORDER[at : at + 5])) for at in (0, 5, 10))


def in_order(body, packs=PACKS):
    for pack in packs:

        def step(_, carry):
            body(carry % 16)
            return carry // 16

        lax.fori_loop(0, 5, step, jnp.int32(pack))


def loop(count, body, start=0):
    def step(index, carry):
        body(index)
        return carry

    lax.fori_loop(start, count, step, jnp.int32(0))


def nn(a, b):
    return lax.dot_general(a, b, (((1,), (0,)), ((), ())), preferred_element_type=F32)


def nt(a, b):
    return lax.dot_general(a, b, (((1,), (1,)), ((), ())), preferred_element_type=F32)


def hot(condition):
    return jnp.where(condition, F32(1), F32(0)).astype(BF16)


def kernel(
    grad_hbm, scores_ref, rows_ref, proj_ref, values_hbm, w_hbm,
    sg_out, vg_out, pg_out,
    gbuf, wg, vh, outbox, chosen_in, contrib_in, chosen, pb, ra, rb, rl, rr, f1, f2,
    vgs, vgr, vgp_s, vgp_r, metar, metas, slotr, slotc, reqs, reqr, sgs, sgr,
    lsem, core_s, core_r, req_s, req_r, val_s, val_r, w1_s, w1_r, wq_s, wq_r, wx_s, wx_r,
    p2_s, p2_r, p1_s, p1_r, p3_s, p3_r, con_s, con_r, f1_s, f1_r, f2_s, f2_r, vx_s, vx_r,
):
    m = lax.axis_index("mem")
    d = lax.axis_index("dp")
    z, y = m // 4, m % 4
    x, c = d // 2, d % 2
    partner = (m, x * 2 + (1 - c))

    def peer_mem(label):
        return ((z + label // 4) % 4) * 4 + (y + label % 4) % 4

    def peer(label):
        return (peer_mem(label), d)

    def xpeer(step):
        return (m, ((x + step) % 4) * 2 + c)

    def remote(src, dst, send, recv, device):
        return pltpu.make_async_remote_copy(
            src_ref=src, dst_ref=dst, send_sem=send, recv_sem=recv, device_id=device, device_id_type=MESH
        )

    local_copies = [pltpu.make_async_copy(grad_hbm, gbuf.at[0], lsem.at[0])]
    for q in range(4):
        block = (x + JORDER[q]) % 4
        local_copies.append(
            pltpu.make_async_copy(
                values_hbm.at[:, pl.ds(pl.multiple_of(block * 256 + c * 128, 128), 128)],
                vh.at[:, pl.ds(q * 128, 128)],
                lsem.at[1 + q],
            )
        )
    w_copies = []
    for p in range(2):
        for q in range(4):
            w_copies.append(
                pltpu.make_async_copy(
                    w_hbm.at[p, (x + JORDER[q]) % 4, c], wg.at[0, p, pl.ds(WROW[JORDER[q]] * 128, 128)], lsem.at[5 + p * 4 + q]
                )
            )
    for copy in w_copies + local_copies:
        copy.start()

    barrier = pltpu.get_barrier_semaphore()
    for label in range(1, 16):
        pl.semaphore_signal(barrier, inc=1, device_id=peer(label), device_id_type=MESH)
    for step in range(1, 4):
        pl.semaphore_signal(barrier, inc=1, device_id=xpeer(step), device_id_type=MESH)
    pl.semaphore_signal(barrier, inc=1, device_id=partner, device_id_type=MESH)

    metar[0] = jnp.concatenate(
        [rows_ref[...].astype(F32), proj_ref[...].astype(F32), scores_ref[...], jnp.zeros((2, 512), F32)], axis=0
    )
    pl.semaphore_wait(barrier, 19)

    meta_copy = remote(metar.at[0], metar.at[1], core_s.at[0], core_r.at[0], partner)
    meta_copy.start()
    for copy in w_copies:
        copy.wait()

    mine = pl.ds(0, 192)

    def stage_one(p, step):
        label = step * 4 if p == 0 else step
        return remote(wg.at[0, p, mine], wg.at[label, p, mine], w1_s.at[p, step], w1_r.at[p, step], peer(label))

    def stage_two(p, source, move):
        to = source + move
        return remote(wg.at[source, p, mine], wg.at[to, p, mine], wq_s.at[p, to], wq_r.at[p, to], peer(move))

    def second_stage(held):
        for step in (1, 3, 2):
            stage_two(0, held * 4, step).start()
            stage_two(1, held, step * 4).start()

    def along_x(label, p, step):
        return remote(
            wg.at[label, p, pl.ds(0, 128)],
            wg.at[label, p, pl.ds(WROW[4 - step] * 128, 128)],
            wx_s.at[label, p, step],
            wx_r.at[label, p, 4 - step],
            xpeer(step),
        )

    def both_ways(label, p):
        for step in (1, 3):
            along_x(label, p, step).start()

    def relay(label):
        up = label % 2
        held = WROW[1] + (WROW[3] - WROW[1]) * up
        return remote(
            wg.at[label, :, pl.ds(pl.multiple_of(held * 128 + 64, 64), 64)],
            wg.at[label, :, pl.ds(WROW[2] * 128 + 64, 64)],
            wx_s.at[label, 0, 2],
            wx_r.at[label, 0, 2],
            xpeer(3 - 2 * up),
        )

    for step in (1, 3, 2):
        for p in range(2):
            stage_one(p, step).start()
    grad_copy = remote(grad_hbm, gbuf.at[1], core_s.at[1], core_r.at[1], partner)
    grad_copy.start()

    reqs[...] = jnp.zeros_like(reqs)
    for k in range(2):
        if k == 1:
            meta_copy.wait_recv()
        flat = metar[k]
        metas[k] = jnp.transpose(jnp.concatenate([flat] * 16, axis=0))
        row = jnp.concatenate([flat[0:1, :], flat[1:2, :]], axis=1).astype(I32)
        owner = row >> 10
        label = ((((owner >> 2) - z) & 3) << 2) | (((owner & 3) - y) & 3)
        hit = label == lax.broadcasted_iota(I32, (16, 1024), 0)
        hits = hot(hit)
        before = []
        for part in range(4):
            upper = lax.broadcasted_iota(I32, (1024, 256), 0) < lax.broadcasted_iota(I32, (1024, 256), 1) + part * 256
            before.append(nn(hits, hot(upper)))
        before = jnp.concatenate(before, axis=1)
        rank = jnp.sum(jnp.where(hit, before, F32(0)), axis=0, keepdims=True)
        slot = label.astype(F32) * 128 + rank
        slotr[k] = jnp.broadcast_to(slot, (8, 1024)).astype(I32)
        slotc[k] = jnp.transpose(jnp.broadcast_to(slot, (128, 1024)))
        rank_column = jnp.transpose(jnp.broadcast_to(rank, (128, 1024)))
        places = hot(rank_column == lax.broadcasted_iota(I32, (1024, 128), 1).astype(F32))
        number = (row & 1023) + 1
        upper_digit = jnp.where(hit, (number >> 5).astype(F32), F32(0)).astype(BF16)
        lower_digit = jnp.where(hit, (number & 31).astype(F32), F32(0)).astype(BF16)
        asked = nn(upper_digit, places) * 32 + nn(lower_digit, places) - 1
        for label_at in range(16):
            reqs[label_at, k : k + 1, :] = asked[label_at : label_at + 1, :]

    def request(label):
        return remote(reqs.at[label], reqr.at[label], req_s.at[label], req_r.at[label], peer(label))

    in_order(lambda label: request(label).start())
    second_stage(0)
    for held in (1, 3, 2):
        for p in range(2):
            stage_one(p, held).wait_recv()
            both_ways(held * 4 if p == 0 else held, p)
        second_stage(held)
    reqr[0] = reqs[0]
    for copy in local_copies:
        copy.wait()

    def value_copy(label, h):
        back = ((z + 4 - label // 4) % 4) * 4 + (y + 4 - label % 4) % 4
        return remote(
            outbox.at[h, :, label], chosen_in.at[h, :, label], val_s.at[h, label], val_r.at[h, label], (back, d)
        )

    def look_up(label, target):
        parts = []
        for k in range(2):
            column = jnp.transpose(jnp.broadcast_to(reqr[label, k : k + 1, :], (128, 128)))
            base = lax.broadcasted_iota(I32, (128, 128), 1).astype(F32)
            parts.append(jnp.concatenate([hot(column == base + 128 * part) for part in range(8)], axis=1))
        found = nn(jnp.concatenate(parts, axis=0), vh[...]).astype(BF16)
        for k in range(2):
            for h in range(2):
                target[h, k, label] = found[k * 128 : (k + 1) * 128, h * 256 : (h + 1) * 256]

    def serve(label):
        request(label).wait_recv()
        look_up(label, outbox)
        value_copy(label, 0).start()

    in_order(serve)
    look_up(0, chosen_in)

    def choose(at, h):
        k, tile = at // 2, at % 2
        column = slotc[k, pl.ds(pl.multiple_of(tile * 512, 512), 512), :]
        base = lax.broadcasted_iota(I32, (512, 128), 1).astype(F32)
        table = jnp.concatenate([hot(column == base + 128 * part) for part in range(16)], axis=1)
        rows = nn(table, chosen_in[h, k].reshape(2048, 256))
        chosen[k, pl.ds(pl.multiple_of(tile * 512, 512), 512), pl.ds(h * 256, 256)] = rows.astype(BF16)

    def mix_half(mt, h):
        half = pl.ds(h * 256, 256)
        for k in range(2):

            def mix(tile):
                here = pl.ds(pl.multiple_of(tile * 128, 128), 128)
                first = chosen[k, here, half].astype(F32)
                second = chosen[k, pl.ds(pl.multiple_of(512 + tile * 128, 128), 128), half].astype(F32)
                for p in range(2):
                    w0 = jnp.where(metas[k, here, 2:3] == p, metas[k, here, 4:5], F32(0))
                    w1 = jnp.where(metas[k, here, 3:4] == p, metas[k, here, 5:6], F32(0))
                    turned = jnp.transpose(w0 * first + w1 * second).astype(BF16)
                    for q in range(2):
                        mt[
                            pl.ds(q * 256 + p * 128, 128),
                            pl.ds(pl.multiple_of(k * 512 + tile * 128, 128), 128),
                        ] = turned[q * 128 : (q + 1) * 128]

            loop(4, mix)

        for a in (0, 2, 1, 3):

            def partial(b):
                columns = pl.ds(pl.multiple_of((((z + a) % 4) * 4 + (y + b) % 4) * 256, 256), 256)
                term = nn(mt[:, :512], gbuf[0, :, columns]) + nn(mt[:, 512:], gbuf[1, :, columns])
                term = term.astype(BF16)
                for q in range(2):
                    pb[JORDER[h * 2 + q], a * 4 + b] = term[q * 256 : (q + 1) * 256]

            loop(4, partial)
            if h == 0:
                two_away(a).start()
            elif a >= 2:
                to_right(a).start()
        if h == 0:
            to_left(0).start()
            to_left(1).start()

    def span(a):
        return pl.ds(a * 4, 4)

    def two_away(a):
        if a < 2:
            return remote(pb.at[2, span(a)], ra.at[span(a)], p2_s.at[a], p2_r.at[a], xpeer(1))
        return remote(pb.at[2, span(a)], rb.at[span(a - 2)], p2_s.at[a], p2_r.at[a], xpeer(3))

    def to_right(a):
        return remote(pb.at[1, span(a)], rl.at[span(a)], p1_s.at[a], p1_r.at[a], xpeer(1))

    def to_left(a):
        return remote(pb.at[3, span(a)], rr.at[span(a)], p3_s.at[a], p3_r.at[a], xpeer(3))

    def values_half(h):
        in_order(lambda label: value_copy(label, h).wait_recv())
        loop(4, lambda at: choose(at, h))
        pl.run_scoped(lambda mt: mix_half(mt, h), pltpu.VMEM((512, 1024), BF16))

    def merge(a):
        two_away(a).wait_recv()
        block, arrived, shift = (1, ra, 0) if a < 2 else (3, rb, 8)

        def add(b):
            at = a * 4 + b
            pb[block, at] = (pb[block, at].astype(F32) + arrived[at - shift].astype(F32)).astype(BF16)

        loop(4, add)
        (to_right(a) if a < 2 else to_left(a)).start()

    def contrib_copy(label, h):
        return remote(
            outbox.at[h, :, label], contrib_in.at[h, :, label], con_s.at[h, label], con_r.at[h, label], peer(label)
        )

    def score_copy():
        return remote(sgs.at[1], sgr, core_s.at[2], core_r.at[2], partner)

    def scope_pick(pr, contrib):
        def columns_of(label):
            return pl.ds(pl.multiple_of(peer_from(label) * 256, 256), 256)

        def peer_from(label):
            return ((z + 4 - label // 4) % 4) * 4 + (y + 4 - label % 4) % 4

        def project(label, j, first=False):
            place = PLACE[j] * 128
            rows = pl.ds(WROW[j] * 128, 128)
            weights = jnp.concatenate([wg[label, 0, rows], wg[label, 1, rows]], axis=0)
            for k in range(2):
                term = nt(gbuf[k, :, columns_of(label)], weights)
                for p in range(2):
                    here = (pl.ds(k * 512, 512), pl.ds(p * 512 + place, 128))
                    part = term[:, p * 128 : (p + 1) * 128]
                    pr[here] = part if first else pr[here] + part

        def picked(k, q, tile):
            here = pl.ds(pl.multiple_of(tile * 128, 128), 128)
            wide = pr[pl.ds(pl.multiple_of(k * 512 + tile * 128, 128), 128), :]
            return jnp.where(metas[k, here, 2 + q : 3 + q] == 0, wide[:, :512], wide[:, 512:])

        def forward(label):
            @pl.when(label % 4 != 0)
            def _():
                stage_two(0, label, 0).wait_recv()
                both_ways(label, 0)

            @pl.when(label // 4 != 0)
            def _():
                stage_two(1, label, 0).wait_recv()
                both_ways(label, 1)

            project(label, 0)

        def pass_on(label):
            for p in range(2):
                for step in (1, 3):
                    along_x(label, p, step).wait_recv()
            relay(label).start()
            for j in (1, 3):
                project(label, j)

        def last(label):
            relay(label).wait_recv()
            project(label, 2)

        grad_copy.wait_recv()
        for j in range(4):
            project(0, j, True)
        in_order(forward)
        in_order(lambda label: value_copy(label, 1).start())
        in_order(pass_on)
        values_half(0)
        in_order(last)

        for k in range(2):

            def pick(tile):
                here = pl.ds(pl.multiple_of(tile * 128, 128), 128)
                for q in range(2):
                    rows = pl.ds(pl.multiple_of(q * 512 + tile * 128, 128), 128)
                    contrib[k, rows, :] = (metas[k, here, 4 + q : 5 + q] * picked(k, q, tile)).astype(BF16)

            loop(4, pick)

        def pack(label, h, target):
            for k in range(2):
                places = lax.broadcasted_iota(I32, (128, 1024), 0) + label * 128
                half = contrib[k, :, pl.ds(h * 256, 256)]
                target[h, k, label] = nn(hot(slotr[k, 0:1, :] == places), half).astype(BF16)

        def send(label, h):
            pack(label, h, outbox)
            contrib_copy(label, h).start()

        in_order(lambda label: value_copy(label, 0).wait_send())
        in_order(lambda label: send(label, 0))
        values_half(1)
        in_order(lambda label: value_copy(label, 1).wait_send())
        in_order(lambda label: send(label, 1))
        for h in range(2):
            pack(0, h, contrib_in)
        for a in (1, 2, 0, 3):
            merge(a)

        for k in range(2):

            def score(tile):
                lanes = lax.broadcasted_iota(I32, (128, 128), 1)
                kept = jnp.zeros((128, 128), F32)
                for q in range(2):
                    rows = pl.ds(pl.multiple_of(q * 512 + tile * 128, 128), 128)
                    total = jnp.sum(picked(k, q, tile) * chosen[k, rows, :].astype(F32), axis=1, keepdims=True)
                    kept = jnp.where(lanes == q, total, kept)
                sgs[k, pl.ds(pl.multiple_of(tile * 128, 128), 128), :] = kept

            loop(4, score)
        score_copy().start()

    pl.run_scoped(scope_pick, pltpu.VMEM((1024, 1024), F32), pltpu.VMEM((2, 1024, 512), BF16))

    def half_rows(p):
        return pl.ds(p * 128, 128)

    def first_z(a):
        return remote(pb.at[0, span(a), half_rows(0)], f1.at[0, a], f1_s.at[0, a, 0], f1_r.at[0, a, 0], peer(a * 4))

    def first_y(a, b):
        return remote(pb.at[0, a * 4 + b, half_rows(1)], f1.at[1, b, a], f1_s.at[1, b, a], f1_r.at[1, b, a], peer(b))

    def then_y(b):
        return remote(pb.at[0, b, half_rows(0)], f2.at[0, b], f2_s.at[0, b], f2_r.at[0, b], peer(b))

    def then_z(a):
        return remote(pb.at[0, a * 4, half_rows(1)], f2.at[1, a], f2_s.at[1, a], f2_r.at[1, a], peer(a * 4))

    def finish_x(order):
        for a in order:
            to_right(a).wait_recv()
            to_left(a).wait_recv()

            def finish(b):
                at = a * 4 + b
                total = pb[0, at].astype(F32) + rl[at].astype(F32) + rr[at].astype(F32)
                pb[0, at] = total.astype(BF16)

            loop(4, finish)
            if a:
                first_z(a).start()
            for b in (1, 3, 2):
                first_y(a, b).start()

    def finish_stage():
        for step in (1, 3, 2):
            first_z(step).wait_recv()
            for a in range(4):
                first_y(a, step).wait_recv()
        for place in (1, 3, 2, 0):
            for p in range(2):
                at = place if p == 0 else place * 4
                total = pb[0, at, half_rows(p), :].astype(F32)
                for step in range(1, 4):
                    total = total + f1[p, step, place].astype(F32)
                pb[0, at, half_rows(p), :] = total.astype(BF16)
            if place:
                then_y(place).start()
                then_z(place).start()

    def vg_copy(step, h):
        return remote(vgs.at[h, step], vgr.at[h, step], vx_s.at[h, step], vx_r.at[h, step], xpeer(step))

    def vg_partner():
        return remote(vgp_s, vgp_r, core_s.at[3], core_r.at[3], partner)

    def scope_values(vg):
        def gather(label, h, first=False):
            half = pl.ds(h * 256, 256)
            parts = []
            for k in range(2):
                places = lax.broadcasted_iota(I32, (1024, 128), 0).astype(F32)
                parts.append(hot(places == reqr[label, k : k + 1, :]))
            rows = jnp.concatenate([contrib_in[h, 0, label], contrib_in[h, 1, label]], axis=0)
            term = nn(jnp.concatenate(parts, axis=1), rows)
            vg[:, half] = term if first else vg[:, half] + term

        for h in range(2):
            gather(0, h, True)

            def arrive(label):
                contrib_copy(label, h).wait_recv()
                gather(label, h)

            in_order(arrive)
            for step in (2, 1, 3):
                rows = pl.ds(pl.multiple_of(((x + step) % 4) * 256, 256), 256)
                vgs[h, step] = vg[rows, pl.ds(h * 256, 256)].astype(BF16)
                vg_copy(step, h).start()
        finish_x((2, 1, 3, 0))
        finish_stage()
        vg[:256, :] = vg[pl.ds(pl.multiple_of(x * 256, 256), 256), :]
        for h in range(2):
            for step in (1, 3, 2):
                vg_copy(step, h).wait_recv()
                for q in range(2):
                    to = pl.ds(PLACE[(JORDER[h * 2 + q] - step) % 4] * 128, 128)
                    vg[:256, to] = vg[:256, to] + vgr[h, step, :, pl.ds(q * 128, 128)].astype(F32)
        vgp_s[...] = vg[pl.ds(pl.multiple_of((1 - c) * 128, 128), 128), :].astype(BF16)
        vg_partner().start()
        mine = vg[pl.ds(pl.multiple_of(c * 128, 128), 128), :].astype(BF16)
        for q in range(4):
            at = pl.multiple_of(((x + JORDER[q]) % 4) * 256 + c * 128, 128)
            vg_out[:, pl.ds(at, 128)] = mine[:, q * 128 : (q + 1) * 128]

    pl.run_scoped(scope_values, pltpu.VMEM((1024, 512), F32))

    for step in (1, 3, 2):
        then_y(step).wait_recv()
        then_z(step).wait_recv()
    for p in range(2):
        total = pb[0, 0, half_rows(p), :].astype(F32)
        for step in range(1, 4):
            total = total + f2[p, step].astype(F32)
        pg_out[p] = total

    score_copy().wait_recv()
    sg_out[...] = jnp.transpose(sgs[0] + sgr[...])[0:2, :]

    vg_partner().wait_recv()
    other = vgp_r[...]
    for q in range(4):
        at = pl.multiple_of(((x + JORDER[q]) % 4) * 256 + (1 - c) * 128, 128)
        vg_out[:, pl.ds(at, 128)] = other[:, q * 128 : (q + 1) * 128]

    meta_copy.wait_send()
    grad_copy.wait_send()
    score_copy().wait_send()
    vg_partner().wait_send()

    def sent(label):
        @pl.when(label % 4 != 0)
        def _():
            stage_two(0, label, 0).wait_send()

        @pl.when(label // 4 != 0)
        def _():
            stage_two(1, label, 0).wait_send()

        request(label).wait_send()
        for h in range(2):
            contrib_copy(label, h).wait_send()
        for p in range(2):
            for step in (1, 3):
                along_x(label, p, step).wait_send()
        relay(label).wait_send()

    loop(16, sent, 1)
    for step in range(1, 4):
        for h in range(2):
            vg_copy(step, h).wait_send()
        first_z(step).wait_send()
        for p in range(2):
            stage_one(p, step).wait_send()
        then_y(step).wait_send()
        then_z(step).wait_send()
        for a in range(4):
            first_y(a, step).wait_send()
    for a in range(4):
        two_away(a).wait_send()
        to_right(a).wait_send()
        to_left(a).wait_send()


def local(grad_out, scores, row_ids, proj_ids, values, proj_w):
    vmem = pl.BlockSpec(memory_space=pltpu.VMEM)
    anywhere = pl.BlockSpec(memory_space=pl.ANY)
    dma = pltpu.SemaphoreType.DMA
    score_grads, value_grads, proj_grads = pl.pallas_call(
        kernel,
        out_shape=(
            jax.ShapeDtypeStruct((2, 512), F32),
            jax.ShapeDtypeStruct((128, 1024), BF16),
            jax.ShapeDtypeStruct((2, 128, 256), F32),
        ),
        in_specs=[anywhere, vmem, vmem, vmem, anywhere, anywhere],
        out_specs=(vmem, vmem, vmem),
        scratch_shapes=[
            pltpu.VMEM((2, 512, 4096), BF16),
            pltpu.VMEM((16, 2, 512, 256), BF16),
            pltpu.VMEM((1024, 512), BF16),
            pltpu.VMEM((2, 2, 16, 128, 256), BF16),
            pltpu.VMEM((2, 2, 16, 128, 256), BF16),
            pltpu.VMEM((2, 2, 16, 128, 256), BF16),
            pltpu.VMEM((2, 1024, 512), BF16),
            pltpu.VMEM((4, 16, 256, 256), BF16),
            pltpu.VMEM((8, 256, 256), BF16),
            pltpu.VMEM((8, 256, 256), BF16),
            pltpu.VMEM((16, 256, 256), BF16),
            pltpu.VMEM((16, 256, 256), BF16),
            pltpu.VMEM((2, 4, 4, 128, 256), BF16),
            pltpu.VMEM((2, 4, 128, 256), BF16),
            pltpu.VMEM((2, 4, 256, 256), BF16),
            pltpu.VMEM((2, 4, 256, 256), BF16),
            pltpu.VMEM((128, 512), BF16),
            pltpu.VMEM((128, 512), BF16),
            pltpu.VMEM((2, 8, 512), F32),
            pltpu.VMEM((2, 512, 128), F32),
            pltpu.VMEM((2, 8, 1024), I32),
            pltpu.VMEM((2, 1024, 128), F32),
            pltpu.VMEM((16, 8, 128), F32),
            pltpu.VMEM((16, 8, 128), F32),
            pltpu.VMEM((2, 512, 128), F32),
            pltpu.VMEM((512, 128), F32),
            dma((13,)),
            dma((4,)),
            dma((4,)),
            dma((16,)),
            dma((16,)),
            dma((2, 16)),
            dma((2, 16)),
            dma((2, 4)),
            dma((2, 4)),
            dma((2, 16)),
            dma((2, 16)),
            dma((16, 2, 4)),
            dma((16, 2, 4)),
            dma((4,)),
            dma((4,)),
            dma((4,)),
            dma((4,)),
            dma((4,)),
            dma((4,)),
            dma((2, 16)),
            dma((2, 16)),
            dma((2, 4, 4)),
            dma((2, 4, 4)),
            dma((2, 4)),
            dma((2, 4)),
            dma((2, 4)),
            dma((2, 4)),
        ],
        compiler_params=pltpu.CompilerParams(
            collective_id=0, has_side_effects=True, vmem_limit_bytes=67043328
        ),
        name="step",
    )(grad_out, scores.T, row_ids.T, proj_ids.T, values, proj_w.reshape(2, 4, 2, 128, 256))
    return score_grads.T, value_grads, proj_grads


def solution(mesh):
    return jax.shard_map(
        local,
        mesh=mesh,
        in_specs=(
            P(("mem", "dp"), None),
            P(("mem", "dp"), None),
            P(("mem", "dp"), None),
            P(("mem", "dp"), None),
            P("mem", None),
            P(None, None, "mem"),
        ),
        out_specs=(P(("mem", "dp"), None), P(("mem", "dp"), None), P(None, "dp", "mem")),
        check_vma=False,
    )
```

```python
import jax
import jax.numpy as jnp
from jax import lax
from jax.experimental import pallas as pl
from jax.experimental.pallas import tpu as pltpu
from jax.sharding import PartitionSpec as P

F32 = jnp.float32
BF16 = jnp.bfloat16
I32 = jnp.int32
MESH = pl.DeviceIdType.MESH
ORDER = (4, 1, 12, 3, 8, 2, 5, 15, 7, 13, 9, 6, 11, 14, 10)
JORDER = (2, 3, 1, 0)
PLACE = (3, 2, 0, 1)
WROW = (0, 2, 1, 3)
PACKS = tuple(sum(label * 16**place for place, label in enumerate(ORDER[at : at + 5])) for at in (0, 5, 10))


def in_order(body, packs=PACKS):
    for pack in packs:

        def step(_, carry):
            body(carry % 16)
            return carry // 16

        lax.fori_loop(0, 5, step, jnp.int32(pack))


def loop(count, body, start=0):
    def step(index, carry):
        body(index)
        return carry

    lax.fori_loop(start, count, step, jnp.int32(0))


def nn(a, b):
    return lax.dot_general(a, b, (((1,), (0,)), ((), ())), preferred_element_type=F32)


def nt(a, b):
    return lax.dot_general(a, b, (((1,), (1,)), ((), ())), preferred_element_type=F32)


def hot(condition):
    return jnp.where(condition, F32(1), F32(0)).astype(BF16)


def kernel(
    grad_hbm, scores_ref, rows_ref, proj_ref, values_hbm, w_hbm,
    sg_out, vg_out, pg_out,
    gbuf, wg, vh, outbox, chosen_in, contrib_in, chosen, pb, ra, rb, rl, rr, f1, f2,
    vgs, vgr, vgp_s, vgp_r, metar, metas, slotr, slotc, reqs, reqr, sgs, sgr,
    lsem, core_s, core_r, out_s, req_r, val_s, val_r, w1_r, wq_r, wx_r, rel_r,
    p2_r, p1_r, p3_r, con_s, con_r, f1_r, f2_r, vx_s, vx_r,
):
    m = lax.axis_index("mem")
    d = lax.axis_index("dp")
    z, y = m // 4, m % 4
    x, c = d // 2, d % 2
    partner = (m, x * 2 + (1 - c))

    def peer_mem(label):
        return ((z + label // 4) % 4) * 4 + (y + label % 4) % 4

    def peer(label):
        return (peer_mem(label), d)

    def xpeer(step):
        return (m, ((x + step) % 4) * 2 + c)

    def remote(src, dst, send, recv, device):
        return pltpu.make_async_remote_copy(
            src_ref=src, dst_ref=dst, send_sem=send, recv_sem=recv, device_id=device, device_id_type=MESH
        )

    local_copies = [pltpu.make_async_copy(grad_hbm, gbuf.at[0], lsem.at[0])]
    for q in range(4):
        block = (x + JORDER[q]) % 4
        local_copies.append(
            pltpu.make_async_copy(
                values_hbm.at[:, pl.ds(pl.multiple_of(block * 256 + c * 128, 128), 128)],
                vh.at[:, pl.ds(q * 128, 128)],
                lsem.at[2],
            )
        )
    w_copies = []
    for p in range(2):
        for q in range(4):
            w_copies.append(
                pltpu.make_async_copy(
                    w_hbm.at[p, (x + JORDER[q]) % 4, c], wg.at[0, p, pl.ds(WROW[JORDER[q]] * 128, 128)], lsem.at[1]
                )
            )
    for copy in w_copies + local_copies:
        copy.start()

    barrier = pltpu.get_barrier_semaphore()
    for label in range(1, 16):
        pl.semaphore_signal(barrier, inc=1, device_id=peer(label), device_id_type=MESH)
    for step in range(1, 4):
        pl.semaphore_signal(barrier, inc=1, device_id=xpeer(step), device_id_type=MESH)
    pl.semaphore_signal(barrier, inc=1, device_id=partner, device_id_type=MESH)

    metar[0] = jnp.concatenate(
        [rows_ref[...].astype(F32), proj_ref[...].astype(F32), scores_ref[...], jnp.zeros((2, 512), F32)], axis=0
    )
    pl.semaphore_wait(barrier, 19)

    meta_copy = remote(metar.at[0], metar.at[1], core_s.at[0], core_r.at[0], partner)
    meta_copy.start()
    pltpu.make_async_copy(wg.at[0], wg.at[0], lsem.at[1]).wait()

    mine = pl.ds(0, 192)

    def stage_one(p, step):
        label = step * 4 if p == 0 else step
        return remote(wg.at[0, p, mine], wg.at[label, p, mine], out_s.at[0], w1_r.at[p, step], peer(label))

    def stage_two(p, source, move):
        to = source + move
        return remote(wg.at[source, p, mine], wg.at[to, p, mine], out_s.at[0], wq_r.at[p, to], peer(move))

    def second_stage(held):
        for step in (1, 3, 2):
            stage_two(0, held * 4, step).start()
            stage_two(1, held, step * 4).start()

    def along_x(label, p, step):
        return remote(
            wg.at[label, p, pl.ds(0, 128)],
            wg.at[label, p, pl.ds(WROW[4 - step] * 128, 128)],
            out_s.at[1],
            wx_r.at[label],
            xpeer(step),
        )

    def from_both(label):
        block = wg.at[label, :, pl.ds(256, 256)]
        return remote(block, block, out_s.at[1], wx_r.at[label], xpeer(1))

    def both_ways(label, p):
        for step in (1, 3):
            along_x(label, p, step).start()

    def relay(label):
        up = label % 2
        held = WROW[1] + (WROW[3] - WROW[1]) * up
        return remote(
            wg.at[label, :, pl.ds(pl.multiple_of(held * 128 + 64, 64), 64)],
            wg.at[label, :, pl.ds(WROW[2] * 128 + 64, 64)],
            out_s.at[2],
            rel_r.at[label],
            xpeer(3 - 2 * up),
        )

    for step in (1, 3, 2):
        for p in range(2):
            stage_one(p, step).start()
    grad_copy = remote(grad_hbm, gbuf.at[1], core_s.at[1], core_r.at[1], partner)
    grad_copy.start()

    reqs[...] = jnp.zeros_like(reqs)
    for k in range(2):
        if k == 1:
            meta_copy.wait_recv()
        flat = metar[k]
        metas[k] = jnp.transpose(jnp.concatenate([flat] * 16, axis=0))
        row = jnp.concatenate([flat[0:1, :], flat[1:2, :]], axis=1).astype(I32)
        owner = row >> 10
        label = ((((owner >> 2) - z) & 3) << 2) | (((owner & 3) - y) & 3)
        hit = label == lax.broadcasted_iota(I32, (16, 1024), 0)
        hits = hot(hit)
        before = []
        for part in range(4):
            upper = lax.broadcasted_iota(I32, (1024, 256), 0) < lax.broadcasted_iota(I32, (1024, 256), 1) + part * 256
            before.append(nn(hits, hot(upper)))
        before = jnp.concatenate(before, axis=1)
        rank = jnp.sum(jnp.where(hit, before, F32(0)), axis=0, keepdims=True)
        slot = label.astype(F32) * 128 + rank
        slotr[k] = jnp.broadcast_to(slot, (8, 1024)).astype(I32)
        slotc[k] = jnp.transpose(jnp.broadcast_to(slot, (128, 1024)))
        rank_column = jnp.transpose(jnp.broadcast_to(rank, (128, 1024)))
        places = hot(rank_column == lax.broadcasted_iota(I32, (1024, 128), 1).astype(F32))
        number = (row & 1023) + 1
        upper_digit = jnp.where(hit, (number >> 5).astype(F32), F32(0)).astype(BF16)
        lower_digit = jnp.where(hit, (number & 31).astype(F32), F32(0)).astype(BF16)
        asked = nn(upper_digit, places) * 32 + nn(lower_digit, places) - 1
        for label_at in range(16):
            reqs[label_at, k : k + 1, :] = asked[label_at : label_at + 1, :]

    def request(label):
        return remote(reqs.at[label], reqr.at[label], out_s.at[3], req_r.at[label], peer(label))

    in_order(lambda label: request(label).start())
    second_stage(0)
    for held in (1, 3, 2):
        for p in range(2):
            stage_one(p, held).wait_recv()
            both_ways(held * 4 if p == 0 else held, p)
        second_stage(held)
    reqr[0] = reqs[0]
    local_copies[0].wait()
    pltpu.make_async_copy(vh, vh, lsem.at[2]).wait()

    def value_copy(label, h):
        back = ((z + 4 - label // 4) % 4) * 4 + (y + 4 - label % 4) % 4
        return remote(
            outbox.at[h, :, label], chosen_in.at[h, :, label], val_s.at[h], val_r.at[h], (back, d)
        )

    def all_values(h):
        every = pl.ds(1, 15)
        return remote(outbox.at[h, :, every], chosen_in.at[h, :, every], val_s.at[h], val_r.at[h], partner)

    def look_up(label, target):
        parts = []
        for k in range(2):
            column = jnp.transpose(jnp.broadcast_to(reqr[label, k : k + 1, :], (128, 128)))
            base = lax.broadcasted_iota(I32, (128, 128), 1).astype(F32)
            parts.append(jnp.concatenate([hot(column == base + 128 * part) for part in range(8)], axis=1))
        found = nn(jnp.concatenate(parts, axis=0), vh[...]).astype(BF16)
        for k in range(2):
            for h in range(2):
                target[h, k, label] = found[k * 128 : (k + 1) * 128, h * 256 : (h + 1) * 256]

    def serve(label):
        request(label).wait_recv()
        look_up(label, outbox)
        value_copy(label, 0).start()

    in_order(serve)
    look_up(0, chosen_in)

    def choose(at, h):
        k, tile = at // 2, at % 2
        column = slotc[k, pl.ds(pl.multiple_of(tile * 512, 512), 512), :]
        base = lax.broadcasted_iota(I32, (512, 128), 1).astype(F32)
        table = jnp.concatenate([hot(column == base + 128 * part) for part in range(16)], axis=1)
        rows = nn(table, chosen_in[h, k].reshape(2048, 256))
        chosen[k, pl.ds(pl.multiple_of(tile * 512, 512), 512), pl.ds(h * 256, 256)] = rows.astype(BF16)

    def mix_half(mt, h):
        half = pl.ds(h * 256, 256)
        for k in range(2):

            def mix(tile):
                here = pl.ds(pl.multiple_of(tile * 128, 128), 128)
                first = chosen[k, here, half].astype(F32)
                second = chosen[k, pl.ds(pl.multiple_of(512 + tile * 128, 128), 128), half].astype(F32)
                for p in range(2):
                    w0 = jnp.where(metas[k, here, 2:3] == p, metas[k, here, 4:5], F32(0))
                    w1 = jnp.where(metas[k, here, 3:4] == p, metas[k, here, 5:6], F32(0))
                    turned = jnp.transpose(w0 * first + w1 * second).astype(BF16)
                    for q in range(2):
                        mt[
                            pl.ds(q * 256 + p * 128, 128),
                            pl.ds(pl.multiple_of(k * 512 + tile * 128, 128), 128),
                        ] = turned[q * 128 : (q + 1) * 128]

            loop(4, mix)

        for a in (0, 2, 1, 3):

            def partial(b):
                columns = pl.ds(pl.multiple_of((((z + a) % 4) * 4 + (y + b) % 4) * 256, 256), 256)
                term = nn(mt[:, :512], gbuf[0, :, columns]) + nn(mt[:, 512:], gbuf[1, :, columns])
                term = term.astype(BF16)
                for q in range(2):
                    pb[JORDER[h * 2 + q], a * 4 + b] = term[q * 256 : (q + 1) * 256]

            loop(4, partial)
            if h == 0:
                two_away(a).start()
            elif a >= 2:
                to_right(a).start()
        if h == 0:
            to_left(0).start()
            to_left(1).start()

    def span(a):
        return pl.ds(a * 4, 4)

    def two_away(a):
        if a < 2:
            return remote(pb.at[2, span(a)], ra.at[span(a)], out_s.at[4], p2_r.at[a], xpeer(1))
        return remote(pb.at[2, span(a)], rb.at[span(a - 2)], out_s.at[4], p2_r.at[a], xpeer(3))

    def to_right(a):
        return remote(pb.at[1, span(a)], rl.at[span(a)], out_s.at[5], p1_r.at[a], xpeer(1))

    def to_left(a):
        return remote(pb.at[3, span(a)], rr.at[span(a)], out_s.at[6], p3_r.at[a], xpeer(3))

    def values_half(h):
        all_values(h).wait_recv()
        loop(4, lambda at: choose(at, h))
        pl.run_scoped(lambda mt: mix_half(mt, h), pltpu.VMEM((512, 1024), BF16))

    def merge(a):
        two_away(a).wait_recv()
        block, arrived, shift = (1, ra, 0) if a < 2 else (3, rb, 8)

        def add(b):
            at = a * 4 + b
            pb[block, at] = (pb[block, at].astype(F32) + arrived[at - shift].astype(F32)).astype(BF16)

        loop(4, add)
        (to_right(a) if a < 2 else to_left(a)).start()

    def contrib_copy(label, h):
        return remote(
            outbox.at[h, :, label], contrib_in.at[h, :, label], con_s.at[h], con_r.at[h, label], peer(label)
        )

    def score_copy():
        return remote(sgs.at[1], sgr, core_s.at[2], core_r.at[2], partner)

    def scope_pick(pr, contrib):
        def columns_of(label):
            return pl.ds(pl.multiple_of(peer_from(label) * 256, 256), 256)

        def peer_from(label):
            return ((z + 4 - label // 4) % 4) * 4 + (y + 4 - label % 4) % 4

        def project(label, j, first=False):
            place = PLACE[j] * 128
            rows = pl.ds(WROW[j] * 128, 128)
            weights = jnp.concatenate([wg[label, 0, rows], wg[label, 1, rows]], axis=0)
            for k in range(2):
                term = nt(gbuf[k, :, columns_of(label)], weights)
                for p in range(2):
                    here = (pl.ds(k * 512, 512), pl.ds(p * 512 + place, 128))
                    part = term[:, p * 128 : (p + 1) * 128]
                    pr[here] = part if first else pr[here] + part

        def picked(k, q, tile):
            here = pl.ds(pl.multiple_of(tile * 128, 128), 128)
            wide = pr[pl.ds(pl.multiple_of(k * 512 + tile * 128, 128), 128), :]
            return jnp.where(metas[k, here, 2 + q : 3 + q] == 0, wide[:, :512], wide[:, 512:])

        def forward(label):
            @pl.when(label % 4 != 0)
            def _():
                stage_two(0, label, 0).wait_recv()
                both_ways(label, 0)

            @pl.when(label // 4 != 0)
            def _():
                stage_two(1, label, 0).wait_recv()
                both_ways(label, 1)

            project(label, 0)

        def pass_on(label):
            from_both(label).wait_recv()
            relay(label).start()
            for j in (1, 3):
                project(label, j)

        def last(label):
            relay(label).wait_recv()
            project(label, 2)

        grad_copy.wait_recv()
        for j in range(4):
            project(0, j, True)
        in_order(forward)
        in_order(lambda label: value_copy(label, 1).start())
        in_order(pass_on)
        values_half(0)
        in_order(last)

        for k in range(2):

            def pick(tile):
                here = pl.ds(pl.multiple_of(tile * 128, 128), 128)
                for q in range(2):
                    rows = pl.ds(pl.multiple_of(q * 512 + tile * 128, 128), 128)
                    contrib[k, rows, :] = (metas[k, here, 4 + q : 5 + q] * picked(k, q, tile)).astype(BF16)

            loop(4, pick)

        def pack(label, h, target):
            for k in range(2):
                places = lax.broadcasted_iota(I32, (128, 1024), 0) + label * 128
                half = contrib[k, :, pl.ds(h * 256, 256)]
                target[h, k, label] = nn(hot(slotr[k, 0:1, :] == places), half).astype(BF16)

        def send(label, h):
            pack(label, h, outbox)
            contrib_copy(label, h).start()

        all_values(0).wait_send()
        in_order(lambda label: send(label, 0))
        values_half(1)
        all_values(1).wait_send()
        in_order(lambda label: send(label, 1))
        for h in range(2):
            pack(0, h, contrib_in)
        for a in (1, 2, 0, 3):
            merge(a)

        for k in range(2):

            def score(tile):
                lanes = lax.broadcasted_iota(I32, (128, 128), 1)
                kept = jnp.zeros((128, 128), F32)
                for q in range(2):
                    rows = pl.ds(pl.multiple_of(q * 512 + tile * 128, 128), 128)
                    total = jnp.sum(picked(k, q, tile) * chosen[k, rows, :].astype(F32), axis=1, keepdims=True)
                    kept = jnp.where(lanes == q, total, kept)
                sgs[k, pl.ds(pl.multiple_of(tile * 128, 128), 128), :] = kept

            loop(4, score)
        score_copy().start()

    pl.run_scoped(scope_pick, pltpu.VMEM((1024, 1024), F32), pltpu.VMEM((2, 1024, 512), BF16))

    def half_rows(p):
        return pl.ds(p * 128, 128)

    def first_z(a):
        return remote(pb.at[0, span(a), half_rows(0)], f1.at[0, a], out_s.at[7], f1_r.at[4], peer(a * 4))

    def first_y(a, b):
        return remote(pb.at[0, a * 4 + b, half_rows(1)], f1.at[1, b, a], out_s.at[8], f1_r.at[a], peer(b))

    def then_y(b):
        return remote(pb.at[0, b, half_rows(0)], f2.at[0, b], out_s.at[9], f2_r.at[0], peer(b))

    def then_z(a):
        return remote(pb.at[0, a * 4, half_rows(1)], f2.at[1, a], out_s.at[10], f2_r.at[1], peer(a * 4))

    others = pl.ds(1, 3)

    def all_first_z():
        block = f1.at[0, others]
        return remote(block, block, out_s.at[7], f1_r.at[4], partner)

    def all_first_y(a):
        block = f1.at[1, others, a]
        return remote(block, block, out_s.at[8], f1_r.at[a], partner)

    def all_then(p):
        block = f2.at[p, others]
        return remote(block, block, out_s.at[9 + p], f2_r.at[p], partner)

    def finish_x(a):
        to_right(a).wait_recv()
        to_left(a).wait_recv()

        def finish(b):
            at = a * 4 + b
            total = pb[0, at].astype(F32) + rl[at].astype(F32) + rr[at].astype(F32)
            pb[0, at] = total.astype(BF16)

        loop(4, finish)
        if a:
            first_z(a).start()
        for b in (1, 3, 2):
            first_y(a, b).start()

    def gathered(p, place):
        total = pb[0, place if p == 0 else place * 4, half_rows(p), :].astype(F32)
        for step in range(1, 4):
            total = total + f1[p, step, place].astype(F32)
        return total

    def finish_all():
        for a in (2, 1, 3):
            finish_x(a)
        for a in (2, 1, 3):
            all_first_y(a).wait_recv()
            pb[0, a * 4, half_rows(1), :] = gathered(1, a).astype(BF16)
            then_z(a).start()
        all_first_z().wait_recv()
        finish_x(0)
        for b in (1, 3, 2):
            pb[0, b, half_rows(0), :] = gathered(0, b).astype(BF16)
            then_y(b).start()

    def vg_copy(step, h):
        return remote(vgs.at[h, step], vgr.at[h, step], vx_s.at[h], vx_r.at[h], xpeer(step))

    def all_vg(h):
        block = vgr.at[h, others]
        return remote(block, block, vx_s.at[h], vx_r.at[h], partner)

    def vg_partner():
        return remote(vgp_s, vgp_r, core_s.at[3], core_r.at[3], partner)

    def scope_values(vg):
        def gather(label, h, first=False):
            half = pl.ds(h * 256, 256)
            parts = []
            for k in range(2):
                places = lax.broadcasted_iota(I32, (1024, 128), 0).astype(F32)
                parts.append(hot(places == reqr[label, k : k + 1, :]))
            rows = jnp.concatenate([contrib_in[h, 0, label], contrib_in[h, 1, label]], axis=0)
            term = nn(jnp.concatenate(parts, axis=1), rows)
            vg[:, half] = term if first else vg[:, half] + term

        for h in range(2):
            gather(0, h, True)

            def arrive(label):
                contrib_copy(label, h).wait_recv()
                gather(label, h)

            in_order(arrive)
            for step in (2, 1, 3):
                rows = pl.ds(pl.multiple_of(((x + step) % 4) * 256, 256), 256)
                vgs[h, step] = vg[rows, pl.ds(h * 256, 256)].astype(BF16)
                vg_copy(step, h).start()
        finish_all()
        vg[:256, :] = vg[pl.ds(pl.multiple_of(x * 256, 256), 256), :]
        for h in range(2):
            all_vg(h).wait_recv()
            for step in (1, 3, 2):
                for q in range(2):
                    to = pl.ds(PLACE[(JORDER[h * 2 + q] - step) % 4] * 128, 128)
                    vg[:256, to] = vg[:256, to] + vgr[h, step, :, pl.ds(q * 128, 128)].astype(F32)
        vgp_s[...] = vg[pl.ds(pl.multiple_of((1 - c) * 128, 128), 128), :].astype(BF16)
        vg_partner().start()
        mine = vg[pl.ds(pl.multiple_of(c * 128, 128), 128), :].astype(BF16)
        for q in range(4):
            at = pl.multiple_of(((x + JORDER[q]) % 4) * 256 + c * 128, 128)
            vg_out[:, pl.ds(at, 128)] = mine[:, q * 128 : (q + 1) * 128]

    pl.run_scoped(scope_values, pltpu.VMEM((1024, 512), F32))

    all_first_y(0).wait_recv()
    for p in range(2):
        all_then(p).wait_recv()
    for p in range(2):
        total = gathered(p, 0)
        for step in range(1, 4):
            total = total + f2[p, step].astype(F32)
        pg_out[p] = total

    score_copy().wait_recv()
    sg_out[...] = jnp.transpose(sgs[0] + sgr[...])[0:2, :]

    vg_partner().wait_recv()
    other = vgp_r[...]
    for q in range(4):
        at = pl.multiple_of(((x + JORDER[q]) % 4) * 256 + (1 - c) * 128, 128)
        vg_out[:, pl.ds(at, 128)] = other[:, q * 128 : (q + 1) * 128]

    meta_copy.wait_send()
    grad_copy.wait_send()
    score_copy().wait_send()
    vg_partner().wait_send()

    def drain(block, sem):
        remote(block, block, sem, w1_r.at[0, 0], partner).wait_send()

    drain(wg.at[pl.ds(1, 15), :, mine], out_s.at[0])
    drain(wg.at[pl.ds(1, 15), :, pl.ds(256, 256)], out_s.at[1])
    drain(wg.at[pl.ds(1, 15), :, pl.ds(192, 64)], out_s.at[2])
    drain(reqs.at[pl.ds(1, 15)], out_s.at[3])
    for block in (2, 1, 3):
        drain(pb.at[block], out_s.at[4 + (2, 1, 3).index(block)])
    drain(f1.at[0, others], out_s.at[7])
    drain(f1.at[1, :, others], out_s.at[8])
    for p in range(2):
        drain(f2.at[p, others], out_s.at[9 + p])
    for h in range(2):
        drain(contrib_in.at[h, :, pl.ds(1, 15)], con_s.at[h])
        drain(vgr.at[h, others], vx_s.at[h])


def hand_over(sg_in, vg_in, pg_in, sg_out, vg_out, pg_out):
    sg_out[...] = sg_in[...]
    vg_out[...] = vg_in[...]
    pg_out[...] = pg_in[...]


def local(grad_out, scores, row_ids, proj_ids, values, proj_w):
    vmem = pl.BlockSpec(memory_space=pltpu.VMEM)
    anywhere = pl.BlockSpec(memory_space=pl.ANY)
    dma = pltpu.SemaphoreType.DMA
    shapes = (
        jax.ShapeDtypeStruct((2, 512), F32),
        jax.ShapeDtypeStruct((128, 1024), BF16),
        jax.ShapeDtypeStruct((2, 128, 256), F32),
    )
    results = pl.pallas_call(
        kernel,
        out_shape=shapes,
        in_specs=[anywhere, vmem, vmem, vmem, anywhere, anywhere],
        out_specs=(vmem, vmem, vmem),
        scratch_shapes=[
            pltpu.VMEM((2, 512, 4096), BF16),
            pltpu.VMEM((16, 2, 512, 256), BF16),
            pltpu.VMEM((1024, 512), BF16),
            pltpu.VMEM((2, 2, 16, 128, 256), BF16),
            pltpu.VMEM((2, 2, 16, 128, 256), BF16),
            pltpu.VMEM((2, 2, 16, 128, 256), BF16),
            pltpu.VMEM((2, 1024, 512), BF16),
            pltpu.VMEM((4, 16, 256, 256), BF16),
            pltpu.VMEM((8, 256, 256), BF16),
            pltpu.VMEM((8, 256, 256), BF16),
            pltpu.VMEM((16, 256, 256), BF16),
            pltpu.VMEM((16, 256, 256), BF16),
            pltpu.VMEM((2, 4, 4, 128, 256), BF16),
            pltpu.VMEM((2, 4, 128, 256), BF16),
            pltpu.VMEM((2, 4, 256, 256), BF16),
            pltpu.VMEM((2, 4, 256, 256), BF16),
            pltpu.VMEM((128, 512), BF16),
            pltpu.VMEM((128, 512), BF16),
            pltpu.VMEM((2, 8, 512), F32),
            pltpu.VMEM((2, 512, 128), F32),
            pltpu.VMEM((2, 8, 1024), I32),
            pltpu.VMEM((2, 1024, 128), F32),
            pltpu.VMEM((16, 8, 128), F32),
            pltpu.VMEM((16, 8, 128), F32),
            pltpu.VMEM((2, 512, 128), F32),
            pltpu.VMEM((512, 128), F32),
            dma((3,)),
            dma((4,)),
            dma((4,)),
            dma((11,)),
            dma((16,)),
            dma((2,)),
            dma((2,)),
            dma((2, 4)),
            dma((2, 16)),
            dma((16,)),
            dma((16,)),
            dma((4,)),
            dma((4,)),
            dma((4,)),
            dma((2,)),
            dma((2, 16)),
            dma((5,)),
            dma((2,)),
            dma((2,)),
            dma((2,)),
        ],
        compiler_params=pltpu.CompilerParams(
            collective_id=0, has_side_effects=True, vmem_limit_bytes=67043328
        ),
        name="step",
    )(grad_out, scores.T, row_ids.T, proj_ids.T, values, proj_w.reshape(2, 4, 2, 128, 256))
    score_grads, value_grads, proj_grads = pl.pallas_call(
        hand_over, out_shape=shapes, in_specs=[vmem] * 3, out_specs=(vmem,) * 3, name="hand_over"
    )(*results)
    return score_grads.T, value_grads, proj_grads


def solution(mesh):
    return jax.shard_map(
        local,
        mesh=mesh,
        in_specs=(
            P(("mem", "dp"), None),
            P(("mem", "dp"), None),
            P(("mem", "dp"), None),
            P(("mem", "dp"), None),
            P("mem", None),
            P(None, None, "mem"),
        ),
        out_specs=(P(("mem", "dp"), None), P(("mem", "dp"), None), P(None, "dp", "mem")),
        check_vma=False,
    )
```

```python
import jax
import jax.numpy as jnp
from jax import lax
from jax.experimental import pallas as pl
from jax.experimental.pallas import tpu as pltpu
from jax.sharding import PartitionSpec as P

F32 = jnp.float32
BF16 = jnp.bfloat16
I32 = jnp.int32
MESH = pl.DeviceIdType.MESH
ORDER = (4, 1, 12, 3, 8, 2, 5, 15, 7, 13, 9, 6, 11, 14, 10)
JORDER = (2, 3, 1, 0)
PLACE = (3, 2, 0, 1)
WROW = (0, 2, 1, 3)
PACKS = tuple(sum(label * 16**place for place, label in enumerate(ORDER[at : at + 5])) for at in (0, 5, 10))


def in_order(body, packs=PACKS):
    for pack in packs:

        def step(_, carry):
            body(carry % 16)
            return carry // 16

        lax.fori_loop(0, 5, step, jnp.int32(pack))


def loop(count, body, start=0):
    def step(index, carry):
        body(index)
        return carry

    lax.fori_loop(start, count, step, jnp.int32(0))


def nn(a, b):
    return lax.dot_general(a, b, (((1,), (0,)), ((), ())), preferred_element_type=F32)


def nt(a, b):
    return lax.dot_general(a, b, (((1,), (1,)), ((), ())), preferred_element_type=F32)


def hot(condition):
    return jnp.where(condition, F32(1), F32(0)).astype(BF16)


def kernel(
    grad_hbm, scores_ref, rows_ref, proj_ref, values_hbm, w_hbm,
    sg_out, vg_out, pg_out,
    gbuf, wg, vh, outbox, chosen_in, contrib_in, chosen, pb, ra, rb, rl, rr, f1, f2,
    vgs, vgr, vgp_s, vgp_r, metar, metas, slotr, slotc, reqs, reqr, sgs, sgr,
    lsem, core_s, core_r, out_s, req_r, val_s, val_r, w1_r, wq_r, wx_r, rel_r,
    p2_r, p1_r, p3_r, con_s, con_r, f1_r, f2_r, vx_s, vx_r,
):
    m = lax.axis_index("mem")
    d = lax.axis_index("dp")
    z, y = m // 4, m % 4
    x, c = d // 2, d % 2
    partner = (m, x * 2 + (1 - c))

    def peer_mem(label):
        return ((z + label // 4) % 4) * 4 + (y + label % 4) % 4

    def peer(label):
        return (peer_mem(label), d)

    def xpeer(step):
        return (m, ((x + step) % 4) * 2 + c)

    def remote(src, dst, send, recv, device):
        return pltpu.make_async_remote_copy(
            src_ref=src, dst_ref=dst, send_sem=send, recv_sem=recv, device_id=device, device_id_type=MESH
        )

    local_copies = [pltpu.make_async_copy(grad_hbm, gbuf.at[0], lsem.at[0])]
    for q in range(4):
        block = (x + JORDER[q]) % 4
        local_copies.append(
            pltpu.make_async_copy(
                values_hbm.at[:, pl.ds(pl.multiple_of(block * 256 + c * 128, 128), 128)],
                vh.at[:, pl.ds(q * 128, 128)],
                lsem.at[2],
            )
        )
    w_copies = []
    for p in range(2):
        for q in range(4):
            w_copies.append(
                pltpu.make_async_copy(
                    w_hbm.at[p, (x + JORDER[q]) % 4, c], wg.at[0, p, pl.ds(WROW[JORDER[q]] * 128, 128)], lsem.at[1]
                )
            )
    for copy in w_copies + local_copies:
        copy.start()

    barrier = pltpu.get_barrier_semaphore()
    for label in range(1, 16):
        pl.semaphore_signal(barrier, inc=1, device_id=peer(label), device_id_type=MESH)
    for step in range(1, 4):
        pl.semaphore_signal(barrier, inc=1, device_id=xpeer(step), device_id_type=MESH)
    pl.semaphore_signal(barrier, inc=1, device_id=partner, device_id_type=MESH)

    metar[0] = jnp.concatenate(
        [rows_ref[...].astype(F32), proj_ref[...].astype(F32), scores_ref[...], jnp.zeros((2, 512), F32)], axis=0
    )
    pl.semaphore_wait(barrier, 19)

    meta_copy = remote(metar.at[0], metar.at[1], core_s.at[0], core_r.at[0], partner)
    meta_copy.start()
    pltpu.make_async_copy(wg.at[0], wg.at[0], lsem.at[1]).wait()

    mine = pl.ds(0, 192)

    def stage_one(p, step):
        label = step * 4 if p == 0 else step
        return remote(wg.at[0, p, mine], wg.at[label, p, mine], out_s.at[0], w1_r.at[p, step], peer(label))

    def stage_two(p, source, move):
        to = source + move
        return remote(wg.at[source, p, mine], wg.at[to, p, mine], out_s.at[0], wq_r.at[p, to], peer(move))

    def second_stage(held):
        for step in (1, 3, 2):
            stage_two(0, held * 4, step).start()
            stage_two(1, held, step * 4).start()

    def along_x(label, p, step):
        return remote(
            wg.at[label, p, pl.ds(0, 128)],
            wg.at[label, p, pl.ds(WROW[4 - step] * 128, 128)],
            out_s.at[1],
            wx_r.at[label],
            xpeer(step),
        )

    def from_both(label):
        block = wg.at[label, :, pl.ds(256, 256)]
        return remote(block, block, out_s.at[1], wx_r.at[label], xpeer(1))

    def both_ways(label, p):
        for step in (1, 3):
            along_x(label, p, step).start()

    def relay(label):
        up = label % 2
        held = WROW[1] + (WROW[3] - WROW[1]) * up
        return remote(
            wg.at[label, :, pl.ds(pl.multiple_of(held * 128 + 64, 64), 64)],
            wg.at[label, :, pl.ds(WROW[2] * 128 + 64, 64)],
            out_s.at[2],
            rel_r.at[label],
            xpeer(3 - 2 * up),
        )

    for step in (1, 3, 2):
        for p in range(2):
            stage_one(p, step).start()
    grad_copy = remote(grad_hbm, gbuf.at[1], core_s.at[1], core_r.at[1], partner)
    grad_copy.start()

    reqs[...] = jnp.zeros_like(reqs)
    for k in range(2):
        if k == 1:
            meta_copy.wait_recv()
        flat = metar[k]
        metas[k] = jnp.transpose(jnp.concatenate([flat] * 16, axis=0))
        row = jnp.concatenate([flat[0:1, :], flat[1:2, :]], axis=1).astype(I32)
        owner = row >> 10
        label = ((((owner >> 2) - z) & 3) << 2) | (((owner & 3) - y) & 3)
        hit = label == lax.broadcasted_iota(I32, (16, 1024), 0)
        hits = hot(hit)
        before = []
        for part in range(4):
            upper = lax.broadcasted_iota(I32, (1024, 256), 0) < lax.broadcasted_iota(I32, (1024, 256), 1) + part * 256
            before.append(nn(hits, hot(upper)))
        before = jnp.concatenate(before, axis=1)
        rank = jnp.sum(jnp.where(hit, before, F32(0)), axis=0, keepdims=True)
        slot = label.astype(F32) * 128 + rank
        slotr[k] = jnp.broadcast_to(slot, (8, 1024)).astype(I32)
        slotc[k] = jnp.transpose(jnp.broadcast_to(slot, (128, 1024)))
        rank_column = jnp.transpose(jnp.broadcast_to(rank, (128, 1024)))
        places = hot(rank_column == lax.broadcasted_iota(I32, (1024, 128), 1).astype(F32))
        number = (row & 1023) + 1
        upper_digit = jnp.where(hit, (number >> 5).astype(F32), F32(0)).astype(BF16)
        lower_digit = jnp.where(hit, (number & 31).astype(F32), F32(0)).astype(BF16)
        asked = nn(upper_digit, places) * 32 + nn(lower_digit, places) - 1
        for label_at in range(16):
            reqs[label_at, k : k + 1, :] = asked[label_at : label_at + 1, :]

    def request(label):
        return remote(reqs.at[label], reqr.at[label], out_s.at[3], req_r.at[label], peer(label))

    in_order(lambda label: request(label).start())
    second_stage(0)
    for held in (1, 3, 2):
        for p in range(2):
            stage_one(p, held).wait_recv()
            both_ways(held * 4 if p == 0 else held, p)
        second_stage(held)
    reqr[0] = reqs[0]
    local_copies[0].wait()
    pltpu.make_async_copy(vh, vh, lsem.at[2]).wait()

    def value_copy(label, h):
        back = ((z + 4 - label // 4) % 4) * 4 + (y + 4 - label % 4) % 4
        return remote(
            outbox.at[h, :, label], chosen_in.at[h, :, label], val_s.at[h], val_r.at[h], (back, d)
        )

    def all_values(h):
        every = pl.ds(1, 15)
        return remote(outbox.at[h, :, every], chosen_in.at[h, :, every], val_s.at[h], val_r.at[h], partner)

    def look_up(label, target):
        parts = []
        for k in range(2):
            column = jnp.transpose(jnp.broadcast_to(reqr[label, k : k + 1, :], (128, 128)))
            base = lax.broadcasted_iota(I32, (128, 128), 1).astype(F32)
            parts.append(jnp.concatenate([hot(column == base + 128 * part) for part in range(8)], axis=1))
        found = nn(jnp.concatenate(parts, axis=0), vh[...]).astype(BF16)
        for k in range(2):
            for h in range(2):
                target[h, k, label] = found[k * 128 : (k + 1) * 128, h * 256 : (h + 1) * 256]

    def serve(label):
        request(label).wait_recv()
        look_up(label, outbox)
        value_copy(label, 0).start()

    in_order(serve)
    look_up(0, chosen_in)

    def choose(at, h):
        k, tile = at // 2, at % 2
        column = slotc[k, pl.ds(pl.multiple_of(tile * 512, 512), 512), :]
        base = lax.broadcasted_iota(I32, (512, 128), 1).astype(F32)
        table = jnp.concatenate([hot(column == base + 128 * part) for part in range(16)], axis=1)
        rows = nn(table, chosen_in[h, k].reshape(2048, 256))
        chosen[k, pl.ds(pl.multiple_of(tile * 512, 512), 512), pl.ds(h * 256, 256)] = rows.astype(BF16)

    def mix_half(mt, h):
        half = pl.ds(h * 256, 256)
        for k in range(2):

            def mix(tile):
                here = pl.ds(pl.multiple_of(tile * 128, 128), 128)
                first = chosen[k, here, half].astype(F32)
                second = chosen[k, pl.ds(pl.multiple_of(512 + tile * 128, 128), 128), half].astype(F32)
                for p in range(2):
                    w0 = jnp.where(metas[k, here, 2:3] == p, metas[k, here, 4:5], F32(0))
                    w1 = jnp.where(metas[k, here, 3:4] == p, metas[k, here, 5:6], F32(0))
                    turned = jnp.transpose(w0 * first + w1 * second).astype(BF16)
                    for q in range(2):
                        mt[
                            pl.ds(q * 256 + p * 128, 128),
                            pl.ds(pl.multiple_of(k * 512 + tile * 128, 128), 128),
                        ] = turned[q * 128 : (q + 1) * 128]

            loop(4, mix)

        order = ((0, 0), (2, 0), (0, 1), (2, 1), (1, 0), (3, 0), (1, 1), (3, 1)) if h == 0 else (
            (2, 0), (2, 1), (3, 0), (3, 1), (0, 0), (0, 1), (1, 0), (1, 1)
        )
        for a, part in order:

            def partial(at):
                b = part * 2 + at
                columns = pl.ds(pl.multiple_of((((z + a) % 4) * 4 + (y + b) % 4) * 256, 256), 256)
                term = nn(mt[:, :512], gbuf[0, :, columns]) + nn(mt[:, 512:], gbuf[1, :, columns])
                term = term.astype(BF16)
                for q in range(2):
                    pb[JORDER[h * 2 + q], a * 4 + b] = term[q * 256 : (q + 1) * 256]

            loop(2, partial)
            if h == 0:
                two_away(a, part).start()
            elif a >= 2:
                to_right(a, part).start()
        if h == 0:
            to_left(0).start()
            to_left(1).start()

    def span(a, part=None):
        return pl.ds(a * 4, 4) if part is None else pl.ds(a * 4 + part * 2, 2)

    def two_away(a, part=None):
        if a < 2:
            return remote(pb.at[2, span(a, part)], ra.at[span(a, part)], out_s.at[4], p2_r.at[a], xpeer(1))
        return remote(pb.at[2, span(a, part)], rb.at[span(a - 2, part)], out_s.at[4], p2_r.at[a], xpeer(3))

    def to_right(a, part=None):
        return remote(pb.at[1, span(a, part)], rl.at[span(a, part)], out_s.at[5], p1_r.at[a], xpeer(1))

    def to_left(a, part=None):
        return remote(pb.at[3, span(a, part)], rr.at[span(a, part)], out_s.at[6], p3_r.at[a], xpeer(3))

    def values_half(h):
        all_values(h).wait_recv()
        loop(4, lambda at: choose(at, h))
        pl.run_scoped(lambda mt: mix_half(mt, h), pltpu.VMEM((512, 1024), BF16))

    def merge(a):
        two_away(a).wait_recv()
        block, arrived, shift = (1, ra, 0) if a < 2 else (3, rb, 8)

        def add(b):
            at = a * 4 + b
            pb[block, at] = (pb[block, at].astype(F32) + arrived[at - shift].astype(F32)).astype(BF16)

        loop(4, add)
        (to_right(a) if a < 2 else to_left(a)).start()

    def contrib_copy(label, h):
        return remote(
            outbox.at[h, :, label], contrib_in.at[h, :, label], con_s.at[h], con_r.at[h, label], peer(label)
        )

    def score_copy():
        return remote(sgs.at[1], sgr, core_s.at[2], core_r.at[2], partner)

    def scope_pick(pr, contrib):
        def columns_of(label):
            return pl.ds(pl.multiple_of(peer_from(label) * 256, 256), 256)

        def peer_from(label):
            return ((z + 4 - label // 4) % 4) * 4 + (y + 4 - label % 4) % 4

        def project(label, j, first=False):
            place = PLACE[j] * 128
            rows = pl.ds(WROW[j] * 128, 128)
            weights = jnp.concatenate([wg[label, 0, rows], wg[label, 1, rows]], axis=0)
            for k in range(2):
                term = nt(gbuf[k, :, columns_of(label)], weights)
                for p in range(2):
                    here = (pl.ds(k * 512, 512), pl.ds(p * 512 + place, 128))
                    part = term[:, p * 128 : (p + 1) * 128]
                    pr[here] = part if first else pr[here] + part

        def picked(k, q, tile):
            here = pl.ds(pl.multiple_of(tile * 128, 128), 128)
            wide = pr[pl.ds(pl.multiple_of(k * 512 + tile * 128, 128), 128), :]
            return jnp.where(metas[k, here, 2 + q : 3 + q] == 0, wide[:, :512], wide[:, 512:])

        def forward(label):
            @pl.when(label % 4 != 0)
            def _():
                stage_two(0, label, 0).wait_recv()
                both_ways(label, 0)

            @pl.when(label // 4 != 0)
            def _():
                stage_two(1, label, 0).wait_recv()
                both_ways(label, 1)

            project(label, 0)

        def pass_on(label):
            from_both(label).wait_recv()
            relay(label).start()
            for j in (1, 3):
                project(label, j)

        def last(label):
            relay(label).wait_recv()
            project(label, 2)

        grad_copy.wait_recv()
        for j in range(4):
            project(0, j, True)
        in_order(forward)
        in_order(lambda label: value_copy(label, 1).start())
        in_order(pass_on)
        values_half(0)
        in_order(last)

        for k in range(2):

            def pick(tile):
                here = pl.ds(pl.multiple_of(tile * 128, 128), 128)
                for q in range(2):
                    rows = pl.ds(pl.multiple_of(q * 512 + tile * 128, 128), 128)
                    contrib[k, rows, :] = (metas[k, here, 4 + q : 5 + q] * picked(k, q, tile)).astype(BF16)

            loop(4, pick)

        def pack(label, h, target):
            for k in range(2):
                places = lax.broadcasted_iota(I32, (128, 1024), 0) + label * 128
                half = contrib[k, :, pl.ds(h * 256, 256)]
                target[h, k, label] = nn(hot(slotr[k, 0:1, :] == places), half).astype(BF16)

        def send(label, h):
            pack(label, h, outbox)
            contrib_copy(label, h).start()

        all_values(0).wait_send()
        in_order(lambda label: send(label, 0))
        values_half(1)
        all_values(1).wait_send()
        in_order(lambda label: send(label, 1))
        for h in range(2):
            pack(0, h, contrib_in)
        for a in (1, 2, 0, 3):
            merge(a)

        for k in range(2):

            def score(tile):
                lanes = lax.broadcasted_iota(I32, (128, 128), 1)
                kept = jnp.zeros((128, 128), F32)
                for q in range(2):
                    rows = pl.ds(pl.multiple_of(q * 512 + tile * 128, 128), 128)
                    total = jnp.sum(picked(k, q, tile) * chosen[k, rows, :].astype(F32), axis=1, keepdims=True)
                    kept = jnp.where(lanes == q, total, kept)
                sgs[k, pl.ds(pl.multiple_of(tile * 128, 128), 128), :] = kept

            loop(4, score)
        score_copy().start()

    pl.run_scoped(scope_pick, pltpu.VMEM((1024, 1024), F32), pltpu.VMEM((2, 1024, 512), BF16))

    def half_rows(p):
        return pl.ds(p * 128, 128)

    def first_z(a):
        return remote(pb.at[0, span(a), half_rows(0)], f1.at[0, a], out_s.at[7], f1_r.at[4], peer(a * 4))

    def first_y(a, b):
        return remote(pb.at[0, a * 4 + b, half_rows(1)], f1.at[1, b, a], out_s.at[8], f1_r.at[a], peer(b))

    def then_y(b):
        return remote(pb.at[0, b, half_rows(0)], f2.at[0, b], out_s.at[9], f2_r.at[0], peer(b))

    def then_z(a):
        return remote(pb.at[0, a * 4, half_rows(1)], f2.at[1, a], out_s.at[10], f2_r.at[1], peer(a * 4))

    others = pl.ds(1, 3)

    def all_first_z():
        block = f1.at[0, others]
        return remote(block, block, out_s.at[7], f1_r.at[4], partner)

    def all_first_y(a):
        block = f1.at[1, others, a]
        return remote(block, block, out_s.at[8], f1_r.at[a], partner)

    def all_then(p):
        block = f2.at[p, others]
        return remote(block, block, out_s.at[9 + p], f2_r.at[p], partner)

    def finish_x(a):
        to_right(a).wait_recv()
        to_left(a).wait_recv()

        def finish(b):
            at = a * 4 + b
            total = pb[0, at].astype(F32) + rl[at].astype(F32) + rr[at].astype(F32)
            pb[0, at] = total.astype(BF16)

        loop(4, finish)
        if a:
            first_z(a).start()
        for b in (1, 3, 2):
            first_y(a, b).start()

    def gathered(p, place):
        total = pb[0, place if p == 0 else place * 4, half_rows(p), :].astype(F32)
        for step in range(1, 4):
            total = total + f1[p, step, place].astype(F32)
        return total

    def finish_all():
        for a in (2, 1, 3):
            finish_x(a)
        for a in (2, 1, 3):
            all_first_y(a).wait_recv()
            pb[0, a * 4, half_rows(1), :] = gathered(1, a).astype(BF16)
            then_z(a).start()
        all_first_z().wait_recv()
        finish_x(0)
        for b in (1, 3, 2):
            pb[0, b, half_rows(0), :] = gathered(0, b).astype(BF16)
            then_y(b).start()

    def vg_copy(step, h):
        return remote(vgs.at[h, step], vgr.at[h, step], vx_s.at[h], vx_r.at[h], xpeer(step))

    def all_vg(h):
        block = vgr.at[h, others]
        return remote(block, block, vx_s.at[h], vx_r.at[h], partner)

    def vg_partner():
        return remote(vgp_s, vgp_r, core_s.at[3], core_r.at[3], partner)

    def scope_values(vg):
        def gather(label, h, first=False):
            half = pl.ds(h * 256, 256)
            parts = []
            for k in range(2):
                places = lax.broadcasted_iota(I32, (1024, 128), 0).astype(F32)
                parts.append(hot(places == reqr[label, k : k + 1, :]))
            rows = jnp.concatenate([contrib_in[h, 0, label], contrib_in[h, 1, label]], axis=0)
            term = nn(jnp.concatenate(parts, axis=1), rows)
            vg[:, half] = term if first else vg[:, half] + term

        for h in range(2):
            gather(0, h, True)

            def arrive(label):
                contrib_copy(label, h).wait_recv()
                gather(label, h)

            in_order(arrive)
            for step in (2, 1, 3):
                rows = pl.ds(pl.multiple_of(((x + step) % 4) * 256, 256), 256)
                vgs[h, step] = vg[rows, pl.ds(h * 256, 256)].astype(BF16)
                vg_copy(step, h).start()
        finish_all()
        vg[:256, :] = vg[pl.ds(pl.multiple_of(x * 256, 256), 256), :]
        for h in range(2):
            all_vg(h).wait_recv()
            for step in (1, 3, 2):
                for q in range(2):
                    to = pl.ds(PLACE[(JORDER[h * 2 + q] - step) % 4] * 128, 128)
                    vg[:256, to] = vg[:256, to] + vgr[h, step, :, pl.ds(q * 128, 128)].astype(F32)
        vgp_s[...] = vg[pl.ds(pl.multiple_of((1 - c) * 128, 128), 128), :].astype(BF16)
        vg_partner().start()
        mine = vg[pl.ds(pl.multiple_of(c * 128, 128), 128), :].astype(BF16)
        for q in range(4):
            at = pl.multiple_of(((x + JORDER[q]) % 4) * 256 + c * 128, 128)
            vg_out[:, pl.ds(at, 128)] = mine[:, q * 128 : (q + 1) * 128]

    pl.run_scoped(scope_values, pltpu.VMEM((1024, 512), F32))

    all_first_y(0).wait_recv()
    for p in range(2):
        all_then(p).wait_recv()
    for p in range(2):
        total = gathered(p, 0)
        for step in range(1, 4):
            total = total + f2[p, step].astype(F32)
        pg_out[p] = total

    score_copy().wait_recv()
    sg_out[...] = jnp.transpose(sgs[0] + sgr[...])[0:2, :]

    vg_partner().wait_recv()
    other = vgp_r[...]
    for q in range(4):
        at = pl.multiple_of(((x + JORDER[q]) % 4) * 256 + (1 - c) * 128, 128)
        vg_out[:, pl.ds(at, 128)] = other[:, q * 128 : (q + 1) * 128]

    meta_copy.wait_send()
    grad_copy.wait_send()
    score_copy().wait_send()
    vg_partner().wait_send()

    def drain(block, sem):
        remote(block, block, sem, w1_r.at[0, 0], partner).wait_send()

    drain(wg.at[pl.ds(1, 15), :, mine], out_s.at[0])
    drain(wg.at[pl.ds(1, 15), :, pl.ds(256, 256)], out_s.at[1])
    drain(wg.at[pl.ds(1, 15), :, pl.ds(192, 64)], out_s.at[2])
    drain(reqs.at[pl.ds(1, 15)], out_s.at[3])
    for block in (2, 1, 3):
        drain(pb.at[block], out_s.at[4 + (2, 1, 3).index(block)])
    drain(f1.at[0, others], out_s.at[7])
    drain(f1.at[1, :, others], out_s.at[8])
    for p in range(2):
        drain(f2.at[p, others], out_s.at[9 + p])
    for h in range(2):
        drain(contrib_in.at[h, :, pl.ds(1, 15)], con_s.at[h])
        drain(vgr.at[h, others], vx_s.at[h])


def hand_over(sg_in, vg_in, pg_in, sg_out, vg_out, pg_out):
    sg_out[...] = sg_in[...]
    vg_out[...] = vg_in[...]
    pg_out[...] = pg_in[...]


def local(grad_out, scores, row_ids, proj_ids, values, proj_w):
    vmem = pl.BlockSpec(memory_space=pltpu.VMEM)
    anywhere = pl.BlockSpec(memory_space=pl.ANY)
    dma = pltpu.SemaphoreType.DMA
    shapes = (
        jax.ShapeDtypeStruct((2, 512), F32),
        jax.ShapeDtypeStruct((128, 1024), BF16),
        jax.ShapeDtypeStruct((2, 128, 256), F32),
    )
    results = pl.pallas_call(
        kernel,
        out_shape=shapes,
        in_specs=[anywhere, vmem, vmem, vmem, anywhere, anywhere],
        out_specs=(vmem, vmem, vmem),
        scratch_shapes=[
            pltpu.VMEM((2, 512, 4096), BF16),
            pltpu.VMEM((16, 2, 512, 256), BF16),
            pltpu.VMEM((1024, 512), BF16),
            pltpu.VMEM((2, 2, 16, 128, 256), BF16),
            pltpu.VMEM((2, 2, 16, 128, 256), BF16),
            pltpu.VMEM((2, 2, 16, 128, 256), BF16),
            pltpu.VMEM((2, 1024, 512), BF16),
            pltpu.VMEM((4, 16, 256, 256), BF16),
            pltpu.VMEM((8, 256, 256), BF16),
            pltpu.VMEM((8, 256, 256), BF16),
            pltpu.VMEM((16, 256, 256), BF16),
            pltpu.VMEM((16, 256, 256), BF16),
            pltpu.VMEM((2, 4, 4, 128, 256), BF16),
            pltpu.VMEM((2, 4, 128, 256), BF16),
            pltpu.VMEM((2, 4, 256, 256), BF16),
            pltpu.VMEM((2, 4, 256, 256), BF16),
            pltpu.VMEM((128, 512), BF16),
            pltpu.VMEM((128, 512), BF16),
            pltpu.VMEM((2, 8, 512), F32),
            pltpu.VMEM((2, 512, 128), F32),
            pltpu.VMEM((2, 8, 1024), I32),
            pltpu.VMEM((2, 1024, 128), F32),
            pltpu.VMEM((16, 8, 128), F32),
            pltpu.VMEM((16, 8, 128), F32),
            pltpu.VMEM((2, 512, 128), F32),
            pltpu.VMEM((512, 128), F32),
            dma((3,)),
            dma((4,)),
            dma((4,)),
            dma((11,)),
            dma((16,)),
            dma((2,)),
            dma((2,)),
            dma((2, 4)),
            dma((2, 16)),
            dma((16,)),
            dma((16,)),
            dma((4,)),
            dma((4,)),
            dma((4,)),
            dma((2,)),
            dma((2, 16)),
            dma((5,)),
            dma((2,)),
            dma((2,)),
            dma((2,)),
        ],
        compiler_params=pltpu.CompilerParams(
            collective_id=0, has_side_effects=True, vmem_limit_bytes=67043328
        ),
        name="step",
    )(grad_out, scores.T, row_ids.T, proj_ids.T, values, proj_w.reshape(2, 4, 2, 128, 256))
    score_grads, value_grads, proj_grads = pl.pallas_call(
        hand_over, out_shape=shapes, in_specs=[vmem] * 3, out_specs=(vmem,) * 3, name="hand_over"
    )(*results)
    return score_grads.T, value_grads, proj_grads


def solution(mesh):
    return jax.shard_map(
        local,
        mesh=mesh,
        in_specs=(
            P(("mem", "dp"), None),
            P(("mem", "dp"), None),
            P(("mem", "dp"), None),
            P(("mem", "dp"), None),
            P("mem", None),
            P(None, None, "mem"),
        ),
        out_specs=(P(("mem", "dp"), None), P(("mem", "dp"), None), P(None, "dp", "mem")),
        check_vma=False,
    )
```

```python
import jax
import jax.numpy as jnp
from jax import lax
from jax.experimental import pallas as pl
from jax.experimental.pallas import tpu as pltpu
from jax.sharding import PartitionSpec as P

F32 = jnp.float32
BF16 = jnp.bfloat16
I32 = jnp.int32
MESH = pl.DeviceIdType.MESH
ORDER = (4, 1, 12, 3, 8, 2, 5, 15, 7, 13, 9, 6, 11, 14, 10)
JORDER = (2, 3, 1, 0)
PLACE = (3, 2, 0, 1)
WROW = (0, 2, 1, 3)
GROUPS = (ORDER[:5], ORDER[5:10], ORDER[10:])
PACKS = tuple(sum(label * 16**place for place, label in enumerate(ORDER[at : at + 5])) for at in (0, 5, 10))


def in_order(body, packs=PACKS):
    for pack in packs:

        def step(_, carry):
            body(carry % 16)
            return carry // 16

        lax.fori_loop(0, 5, step, jnp.int32(pack))


def loop(count, body, start=0):
    def step(index, carry):
        body(index)
        return carry

    lax.fori_loop(start, count, step, jnp.int32(0))


def nn(a, b):
    return lax.dot_general(a, b, (((1,), (0,)), ((), ())), preferred_element_type=F32)


def nt(a, b):
    return lax.dot_general(a, b, (((1,), (1,)), ((), ())), preferred_element_type=F32)


def hot(condition):
    return jnp.where(condition, F32(1), F32(0)).astype(BF16)


def kernel(
    grad_hbm, scores_ref, rows_ref, proj_ref, values_hbm, w_hbm,
    sg_out, vg_out, pg_out,
    gbuf, wg, vh, outbox, chosen_in, contrib_in, chosen, pb, ra, rb, rl, rr, f1, f2,
    vgs, vgr, vgp_s, vgp_r, metar, metas, slotr, slotc, reqs, reqr, sgs, sgr,
    lsem, core_s, core_r, out_s, req_r, val_s, val_r, w1_r, wq_r, wx_r, rel_r,
    p2_r, p1_r, p3_r, con_s, con_r, f1_r, f2_r, vx_s, vx_r,
):
    m = lax.axis_index("mem")
    d = lax.axis_index("dp")
    z, y = m // 4, m % 4
    x, c = d // 2, d % 2
    partner = (m, x * 2 + (1 - c))

    def peer_mem(label):
        return ((z + label // 4) % 4) * 4 + (y + label % 4) % 4

    def peer(label):
        return (peer_mem(label), d)

    def xpeer(step):
        return (m, ((x + step) % 4) * 2 + c)

    def remote(src, dst, send, recv, device):
        return pltpu.make_async_remote_copy(
            src_ref=src, dst_ref=dst, send_sem=send, recv_sem=recv, device_id=device, device_id_type=MESH
        )

    local_copies = [pltpu.make_async_copy(grad_hbm, gbuf.at[0], lsem.at[0])]
    for q in range(4):
        block = (x + JORDER[q]) % 4
        local_copies.append(
            pltpu.make_async_copy(
                values_hbm.at[:, pl.ds(pl.multiple_of(block * 256 + c * 128, 128), 128)],
                vh.at[:, pl.ds(q * 128, 128)],
                lsem.at[2],
            )
        )
    w_copies = []
    for p in range(2):
        for q in range(4):
            w_copies.append(
                pltpu.make_async_copy(
                    w_hbm.at[p, (x + JORDER[q]) % 4, c], wg.at[0, p, pl.ds(WROW[JORDER[q]] * 128, 128)], lsem.at[1]
                )
            )
    for copy in w_copies + local_copies:
        copy.start()

    barrier = pltpu.get_barrier_semaphore()
    for label in range(1, 16):
        pl.semaphore_signal(barrier, inc=1, device_id=peer(label), device_id_type=MESH)
    for step in range(1, 4):
        pl.semaphore_signal(barrier, inc=1, device_id=xpeer(step), device_id_type=MESH)
    pl.semaphore_signal(barrier, inc=1, device_id=partner, device_id_type=MESH)

    metar[0] = jnp.concatenate(
        [rows_ref[...].astype(F32), proj_ref[...].astype(F32), scores_ref[...], jnp.zeros((2, 512), F32)], axis=0
    )
    pl.semaphore_wait(barrier, 19)

    meta_copy = remote(metar.at[0], metar.at[1], core_s.at[0], core_r.at[0], partner)
    meta_copy.start()
    pltpu.make_async_copy(wg.at[0], wg.at[0], lsem.at[1]).wait()

    mine = pl.ds(0, 192)

    def stage_one(p, step):
        label = step * 4 if p == 0 else step
        return remote(wg.at[0, p, mine], wg.at[label, p, mine], out_s.at[0], w1_r.at[p, step], peer(label))

    def stage_two(p, source, move):
        to = source + move
        return remote(wg.at[source, p, mine], wg.at[to, p, mine], out_s.at[0], wq_r.at[p, to], peer(move))

    def second_stage(held):
        for step in (1, 3, 2):
            stage_two(0, held * 4, step).start()
            stage_two(1, held, step * 4).start()

    def along_x(label, p, step):
        return remote(
            wg.at[label, p, pl.ds(0, 128)],
            wg.at[label, p, pl.ds(WROW[4 - step] * 128, 128)],
            out_s.at[1],
            wx_r.at[label],
            xpeer(step),
        )

    def from_both(label):
        block = wg.at[label, :, pl.ds(256, 256)]
        return remote(block, block, out_s.at[1], wx_r.at[label], xpeer(1))

    def both_ways(label, p):
        for step in (1, 3):
            along_x(label, p, step).start()

    def relay(label):
        up = label % 2
        held = WROW[1] + (WROW[3] - WROW[1]) * up
        return remote(
            wg.at[label, :, pl.ds(pl.multiple_of(held * 128 + 64, 64), 64)],
            wg.at[label, :, pl.ds(WROW[2] * 128 + 64, 64)],
            out_s.at[2],
            rel_r.at[label],
            xpeer(3 - 2 * up),
        )

    for step in (1, 3, 2):
        for p in range(2):
            stage_one(p, step).start()
    grad_copy = remote(grad_hbm, gbuf.at[1], core_s.at[1], core_r.at[1], partner)
    grad_copy.start()

    reqs[...] = jnp.zeros_like(reqs)
    for k in range(2):
        if k == 1:
            meta_copy.wait_recv()
        flat = metar[k]
        metas[k] = jnp.transpose(jnp.concatenate([flat] * 16, axis=0))
        row = jnp.concatenate([flat[0:1, :], flat[1:2, :]], axis=1).astype(I32)
        owner = row >> 10
        label = ((((owner >> 2) - z) & 3) << 2) | (((owner & 3) - y) & 3)
        hit = label == lax.broadcasted_iota(I32, (16, 1024), 0)
        hits = hot(hit)
        before = []
        for part in range(4):
            upper = lax.broadcasted_iota(I32, (1024, 256), 0) < lax.broadcasted_iota(I32, (1024, 256), 1) + part * 256
            before.append(nn(hits, hot(upper)))
        before = jnp.concatenate(before, axis=1)
        rank = jnp.sum(jnp.where(hit, before, F32(0)), axis=0, keepdims=True)
        slot = label.astype(F32) * 128 + rank
        slotr[k] = jnp.broadcast_to(slot, (8, 1024)).astype(I32)
        slotc[k] = jnp.transpose(jnp.broadcast_to(slot, (128, 1024)))
        rank_column = jnp.transpose(jnp.broadcast_to(rank, (128, 1024)))
        places = hot(rank_column == lax.broadcasted_iota(I32, (1024, 128), 1).astype(F32))
        number = (row & 1023) + 1
        upper_digit = jnp.where(hit, (number >> 5).astype(F32), F32(0)).astype(BF16)
        lower_digit = jnp.where(hit, (number & 31).astype(F32), F32(0)).astype(BF16)
        asked = nn(upper_digit, places) * 32 + nn(lower_digit, places) - 1
        for label_at in range(16):
            reqs[label_at, k : k + 1, :] = asked[label_at : label_at + 1, :]

    def request(label):
        return remote(reqs.at[label], reqr.at[label], out_s.at[3], req_r.at[label], peer(label))

    in_order(lambda label: request(label).start())
    second_stage(0)
    for held in (1, 3, 2):
        for p in range(2):
            stage_one(p, held).wait_recv()
            both_ways(held * 4 if p == 0 else held, p)
        second_stage(held)
    reqr[0] = reqs[0]
    local_copies[0].wait()
    pltpu.make_async_copy(vh, vh, lsem.at[2]).wait()

    def value_copy(label, h):
        back = ((z + 4 - label // 4) % 4) * 4 + (y + 4 - label % 4) % 4
        return remote(
            outbox.at[h, :, label], chosen_in.at[h, :, label], val_s.at[h], val_r.at[h], (back, d)
        )

    def all_values(h):
        every = pl.ds(1, 15)
        return remote(outbox.at[h, :, every], chosen_in.at[h, :, every], val_s.at[h], val_r.at[h], partner)

    def look_up(label, target):
        parts = []
        for k in range(2):
            column = jnp.transpose(jnp.broadcast_to(reqr[label, k : k + 1, :], (128, 128)))
            base = lax.broadcasted_iota(I32, (128, 128), 1).astype(F32)
            parts.append(jnp.concatenate([hot(column == base + 128 * part) for part in range(8)], axis=1))
        found = nn(jnp.concatenate(parts, axis=0), vh[...]).astype(BF16)
        for k in range(2):
            for h in range(2):
                target[h, k, label] = found[k * 128 : (k + 1) * 128, h * 256 : (h + 1) * 256]

    def serve(label):
        request(label).wait_recv()
        look_up(label, outbox)
        value_copy(label, 0).start()

    in_order(serve)
    look_up(0, chosen_in)

    def choose(at, h):
        k, tile = at // 2, at % 2
        column = slotc[k, pl.ds(pl.multiple_of(tile * 512, 512), 512), :]
        base = lax.broadcasted_iota(I32, (512, 128), 1).astype(F32)
        table = jnp.concatenate([hot(column == base + 128 * part) for part in range(16)], axis=1)
        rows = nn(table, chosen_in[h, k].reshape(2048, 256))
        chosen[k, pl.ds(pl.multiple_of(tile * 512, 512), 512), pl.ds(h * 256, 256)] = rows.astype(BF16)

    def mix_half(mt, h):
        half = pl.ds(h * 256, 256)
        for k in range(2):

            def mix(tile):
                here = pl.ds(pl.multiple_of(tile * 128, 128), 128)
                first = chosen[k, here, half].astype(F32)
                second = chosen[k, pl.ds(pl.multiple_of(512 + tile * 128, 128), 128), half].astype(F32)
                for p in range(2):
                    w0 = jnp.where(metas[k, here, 2:3] == p, metas[k, here, 4:5], F32(0))
                    w1 = jnp.where(metas[k, here, 3:4] == p, metas[k, here, 5:6], F32(0))
                    turned = jnp.transpose(w0 * first + w1 * second).astype(BF16)
                    for q in range(2):
                        mt[
                            pl.ds(q * 256 + p * 128, 128),
                            pl.ds(pl.multiple_of(k * 512 + tile * 128, 128), 128),
                        ] = turned[q * 128 : (q + 1) * 128]

            loop(4, mix)

        order = ((0, 0), (2, 0), (0, 1), (2, 1), (1, 0), (3, 0), (1, 1), (3, 1)) if h == 0 else (
            (2, 0), (2, 1), (3, 0), (3, 1), (0, 0), (0, 1), (1, 0), (1, 1)
        )
        for a, part in order:

            def partial(at):
                b = part * 2 + at
                columns = pl.ds(pl.multiple_of((((z + a) % 4) * 4 + (y + b) % 4) * 256, 256), 256)
                term = nn(mt[:, :512], gbuf[0, :, columns]) + nn(mt[:, 512:], gbuf[1, :, columns])
                term = term.astype(BF16)
                for q in range(2):
                    pb[JORDER[h * 2 + q], a * 4 + b] = term[q * 256 : (q + 1) * 256]

            loop(2, partial)
            if h == 0:
                two_away(a, part).start()
            elif a >= 2:
                to_right(a, part).start()
        if h == 0:
            to_left(0).start()
            to_left(1).start()

    def span(a, part=None):
        return pl.ds(a * 4, 4) if part is None else pl.ds(a * 4 + part * 2, 2)

    def two_away(a, part=None):
        if a < 2:
            return remote(pb.at[2, span(a, part)], ra.at[span(a, part)], out_s.at[4], p2_r.at[a], xpeer(1))
        return remote(pb.at[2, span(a, part)], rb.at[span(a - 2, part)], out_s.at[4], p2_r.at[a], xpeer(3))

    def to_right(a, part=None):
        return remote(pb.at[1, span(a, part)], rl.at[span(a, part)], out_s.at[5], p1_r.at[a], xpeer(1))

    def to_left(a, part=None):
        return remote(pb.at[3, span(a, part)], rr.at[span(a, part)], out_s.at[6], p3_r.at[a], xpeer(3))

    def values_half(h):
        all_values(h).wait_recv()
        loop(4, lambda at: choose(at, h))
        pl.run_scoped(lambda mt: mix_half(mt, h), pltpu.VMEM((512, 1024), BF16))

    def merge(a):
        two_away(a).wait_recv()
        block, arrived, shift = (1, ra, 0) if a < 2 else (3, rb, 8)

        def add(b):
            at = a * 4 + b
            pb[block, at] = (pb[block, at].astype(F32) + arrived[at - shift].astype(F32)).astype(BF16)

        loop(4, add)
        (to_right(a) if a < 2 else to_left(a)).start()

    def contrib_copy(label, h):
        return remote(
            outbox.at[h, :, label], contrib_in.at[h, :, label], con_s.at[h], con_r.at[h, label], peer(label)
        )

    def score_copy():
        return remote(sgs.at[1], sgr, core_s.at[2], core_r.at[2], partner)

    def scope_pick(pr, contrib):
        def columns_of(label):
            return pl.ds(pl.multiple_of(peer_from(label) * 256, 256), 256)

        def peer_from(label):
            return ((z + 4 - label // 4) % 4) * 4 + (y + 4 - label % 4) % 4

        def project(label, j, first=False):
            place = PLACE[j] * 128
            rows = pl.ds(WROW[j] * 128, 128)
            weights = jnp.concatenate([wg[label, 0, rows], wg[label, 1, rows]], axis=0)
            for k in range(2):
                term = nt(gbuf[k, :, columns_of(label)], weights)
                for p in range(2):
                    here = (pl.ds(k * 512, 512), pl.ds(p * 512 + place, 128))
                    part = term[:, p * 128 : (p + 1) * 128]
                    pr[here] = part if first else pr[here] + part

        def picked(k, q, tile):
            here = pl.ds(pl.multiple_of(tile * 128, 128), 128)
            wide = pr[pl.ds(pl.multiple_of(k * 512 + tile * 128, 128), 128), :]
            return jnp.where(metas[k, here, 2 + q : 3 + q] == 0, wide[:, :512], wide[:, 512:])

        def forward(label):
            @pl.when(label % 4 != 0)
            def _():
                stage_two(0, label, 0).wait_recv()
                both_ways(label, 0)

            @pl.when(label // 4 != 0)
            def _():
                stage_two(1, label, 0).wait_recv()
                both_ways(label, 1)

            project(label, 0)

        def pass_on(label):
            from_both(label).wait_recv()
            relay(label).start()
            for j in (1, 3):
                project(label, j)

        def last(labels):
            for label in labels:
                relay(label).wait_recv()
            place, rows = PLACE[2] * 128, pl.ds(WROW[2] * 128, 128)
            for k in range(2):
                total = jnp.zeros((512, 256), F32)
                for label in labels:
                    weights = jnp.concatenate([wg[label, 0, rows], wg[label, 1, rows]], axis=0)
                    total = total + nt(gbuf[k, :, columns_of(label)], weights)
                for p in range(2):
                    here = (pl.ds(k * 512, 512), pl.ds(p * 512 + place, 128))
                    pr[here] = pr[here] + total[:, p * 128 : (p + 1) * 128]

        grad_copy.wait_recv()
        for j in range(4):
            project(0, j, True)
        in_order(forward)
        in_order(lambda label: value_copy(label, 1).start())
        in_order(pass_on)
        values_half(0)
        for labels in GROUPS:
            last(labels)

        for k in range(2):

            def pick(tile):
                here = pl.ds(pl.multiple_of(tile * 128, 128), 128)
                for q in range(2):
                    rows = pl.ds(pl.multiple_of(q * 512 + tile * 128, 128), 128)
                    contrib[k, rows, :] = (metas[k, here, 4 + q : 5 + q] * picked(k, q, tile)).astype(BF16)

            loop(4, pick)

        def pack(label, h, target):
            for k in range(2):
                places = lax.broadcasted_iota(I32, (128, 1024), 0) + label * 128
                half = contrib[k, :, pl.ds(h * 256, 256)]
                target[h, k, label] = nn(hot(slotr[k, 0:1, :] == places), half).astype(BF16)

        def send(label, h):
            pack(label, h, outbox)
            contrib_copy(label, h).start()

        all_values(0).wait_send()
        in_order(lambda label: send(label, 0))
        values_half(1)
        all_values(1).wait_send()
        in_order(lambda label: send(label, 1))
        for h in range(2):
            pack(0, h, contrib_in)
        for a in (1, 2, 0, 3):
            merge(a)

        for k in range(2):

            def score(tile):
                lanes = lax.broadcasted_iota(I32, (128, 128), 1)
                kept = jnp.zeros((128, 128), F32)
                for q in range(2):
                    rows = pl.ds(pl.multiple_of(q * 512 + tile * 128, 128), 128)
                    total = jnp.sum(picked(k, q, tile) * chosen[k, rows, :].astype(F32), axis=1, keepdims=True)
                    kept = jnp.where(lanes == q, total, kept)
                sgs[k, pl.ds(pl.multiple_of(tile * 128, 128), 128), :] = kept

            loop(4, score)
        score_copy().start()

    pl.run_scoped(scope_pick, pltpu.VMEM((1024, 1024), F32), pltpu.VMEM((2, 1024, 512), BF16))

    def half_rows(p):
        return pl.ds(p * 128, 128)

    def first_z(a):
        return remote(pb.at[0, span(a), half_rows(0)], f1.at[0, a], out_s.at[7], f1_r.at[4], peer(a * 4))

    def first_y(a, b):
        return remote(pb.at[0, a * 4 + b, half_rows(1)], f1.at[1, b, a], out_s.at[8], f1_r.at[a], peer(b))

    def then_y(b):
        return remote(pb.at[0, b, half_rows(0)], f2.at[0, b], out_s.at[9], f2_r.at[0], peer(b))

    def then_z(a):
        return remote(pb.at[0, a * 4, half_rows(1)], f2.at[1, a], out_s.at[10], f2_r.at[1], peer(a * 4))

    others = pl.ds(1, 3)

    def all_first_z():
        block = f1.at[0, others]
        return remote(block, block, out_s.at[7], f1_r.at[4], partner)

    def all_first_y(a):
        block = f1.at[1, others, a]
        return remote(block, block, out_s.at[8], f1_r.at[a], partner)

    def all_then(p):
        block = f2.at[p, others]
        return remote(block, block, out_s.at[9 + p], f2_r.at[p], partner)

    def finish_x(a):
        to_right(a).wait_recv()
        to_left(a).wait_recv()

        def finish(b):
            at = a * 4 + b
            total = pb[0, at].astype(F32) + rl[at].astype(F32) + rr[at].astype(F32)
            pb[0, at] = total.astype(BF16)

        loop(4, finish)
        if a:
            first_z(a).start()
        for b in (1, 3, 2):
            first_y(a, b).start()

    def gathered(p, place):
        total = pb[0, place if p == 0 else place * 4, half_rows(p), :].astype(F32)
        for step in range(1, 4):
            total = total + f1[p, step, place].astype(F32)
        return total

    def finish_all():
        for a in (2, 1, 3):
            finish_x(a)
        for a in (2, 1, 3):
            all_first_y(a).wait_recv()
            pb[0, a * 4, half_rows(1), :] = gathered(1, a).astype(BF16)
            then_z(a).start()
        all_first_z().wait_recv()
        finish_x(0)
        for b in (1, 3, 2):
            pb[0, b, half_rows(0), :] = gathered(0, b).astype(BF16)
            then_y(b).start()

    def vg_copy(step, h):
        return remote(vgs.at[h, step], vgr.at[h, step], vx_s.at[h], vx_r.at[h], xpeer(step))

    def all_vg(h):
        block = vgr.at[h, others]
        return remote(block, block, vx_s.at[h], vx_r.at[h], partner)

    def vg_partner():
        return remote(vgp_s, vgp_r, core_s.at[3], core_r.at[3], partner)

    def scope_values(vg):
        def gather(label, h, first=False):
            half = pl.ds(h * 256, 256)
            parts = []
            for k in range(2):
                places = lax.broadcasted_iota(I32, (1024, 128), 0).astype(F32)
                parts.append(hot(places == reqr[label, k : k + 1, :]))
            rows = jnp.concatenate([contrib_in[h, 0, label], contrib_in[h, 1, label]], axis=0)
            term = nn(jnp.concatenate(parts, axis=1), rows)
            vg[:, half] = term if first else vg[:, half] + term

        for h in range(2):
            gather(0, h, True)

            def arrive(label):
                contrib_copy(label, h).wait_recv()
                gather(label, h)

            in_order(arrive)
            for step in (2, 1, 3):
                rows = pl.ds(pl.multiple_of(((x + step) % 4) * 256, 256), 256)
                vgs[h, step] = vg[rows, pl.ds(h * 256, 256)].astype(BF16)
                vg_copy(step, h).start()
        finish_all()
        vg[:256, :] = vg[pl.ds(pl.multiple_of(x * 256, 256), 256), :]
        for h in range(2):
            all_vg(h).wait_recv()
            for step in (1, 3, 2):
                for q in range(2):
                    to = pl.ds(PLACE[(JORDER[h * 2 + q] - step) % 4] * 128, 128)
                    vg[:256, to] = vg[:256, to] + vgr[h, step, :, pl.ds(q * 128, 128)].astype(F32)
        vgp_s[...] = vg[pl.ds(pl.multiple_of((1 - c) * 128, 128), 128), :].astype(BF16)
        vg_partner().start()
        mine = vg[pl.ds(pl.multiple_of(c * 128, 128), 128), :].astype(BF16)
        for q in range(4):
            at = pl.multiple_of(((x + JORDER[q]) % 4) * 256 + c * 128, 128)
            vg_out[:, pl.ds(at, 128)] = mine[:, q * 128 : (q + 1) * 128]

    pl.run_scoped(scope_values, pltpu.VMEM((1024, 512), F32))

    all_first_y(0).wait_recv()
    for p in range(2):
        all_then(p).wait_recv()
    for p in range(2):
        total = gathered(p, 0)
        for step in range(1, 4):
            total = total + f2[p, step].astype(F32)
        pg_out[p] = total

    score_copy().wait_recv()
    sg_out[...] = jnp.transpose(sgs[0] + sgr[...])[0:2, :]

    vg_partner().wait_recv()
    other = vgp_r[...]
    for q in range(4):
        at = pl.multiple_of(((x + JORDER[q]) % 4) * 256 + (1 - c) * 128, 128)
        vg_out[:, pl.ds(at, 128)] = other[:, q * 128 : (q + 1) * 128]

    meta_copy.wait_send()
    grad_copy.wait_send()
    score_copy().wait_send()
    vg_partner().wait_send()

    def drain(block, sem):
        remote(block, block, sem, w1_r.at[0, 0], partner).wait_send()

    drain(wg.at[pl.ds(1, 15), :, mine], out_s.at[0])
    drain(wg.at[pl.ds(1, 15), :, pl.ds(256, 256)], out_s.at[1])
    drain(wg.at[pl.ds(1, 15), :, pl.ds(192, 64)], out_s.at[2])
    drain(reqs.at[pl.ds(1, 15)], out_s.at[3])
    for block in (2, 1, 3):
        drain(pb.at[block], out_s.at[4 + (2, 1, 3).index(block)])
    drain(f1.at[0, others], out_s.at[7])
    drain(f1.at[1, :, others], out_s.at[8])
    for p in range(2):
        drain(f2.at[p, others], out_s.at[9 + p])
    for h in range(2):
        drain(contrib_in.at[h, :, pl.ds(1, 15)], con_s.at[h])
        drain(vgr.at[h, others], vx_s.at[h])


def hand_over(sg_in, vg_in, pg_in, sg_out, vg_out, pg_out):
    sg_out[...] = sg_in[...]
    vg_out[...] = vg_in[...]
    pg_out[...] = pg_in[...]


def local(grad_out, scores, row_ids, proj_ids, values, proj_w):
    vmem = pl.BlockSpec(memory_space=pltpu.VMEM)
    anywhere = pl.BlockSpec(memory_space=pl.ANY)
    dma = pltpu.SemaphoreType.DMA
    shapes = (
        jax.ShapeDtypeStruct((2, 512), F32),
        jax.ShapeDtypeStruct((128, 1024), BF16),
        jax.ShapeDtypeStruct((2, 128, 256), F32),
    )
    results = pl.pallas_call(
        kernel,
        out_shape=shapes,
        in_specs=[anywhere, vmem, vmem, vmem, anywhere, anywhere],
        out_specs=(vmem, vmem, vmem),
        scratch_shapes=[
            pltpu.VMEM((2, 512, 4096), BF16),
            pltpu.VMEM((16, 2, 512, 256), BF16),
            pltpu.VMEM((1024, 512), BF16),
            pltpu.VMEM((2, 2, 16, 128, 256), BF16),
            pltpu.VMEM((2, 2, 16, 128, 256), BF16),
            pltpu.VMEM((2, 2, 16, 128, 256), BF16),
            pltpu.VMEM((2, 1024, 512), BF16),
            pltpu.VMEM((4, 16, 256, 256), BF16),
            pltpu.VMEM((8, 256, 256), BF16),
            pltpu.VMEM((8, 256, 256), BF16),
            pltpu.VMEM((16, 256, 256), BF16),
            pltpu.VMEM((16, 256, 256), BF16),
            pltpu.VMEM((2, 4, 4, 128, 256), BF16),
            pltpu.VMEM((2, 4, 128, 256), BF16),
            pltpu.VMEM((2, 4, 256, 256), BF16),
            pltpu.VMEM((2, 4, 256, 256), BF16),
            pltpu.VMEM((128, 512), BF16),
            pltpu.VMEM((128, 512), BF16),
            pltpu.VMEM((2, 8, 512), F32),
            pltpu.VMEM((2, 512, 128), F32),
            pltpu.VMEM((2, 8, 1024), I32),
            pltpu.VMEM((2, 1024, 128), F32),
            pltpu.VMEM((16, 8, 128), F32),
            pltpu.VMEM((16, 8, 128), F32),
            pltpu.VMEM((2, 512, 128), F32),
            pltpu.VMEM((512, 128), F32),
            dma((3,)),
            dma((4,)),
            dma((4,)),
            dma((11,)),
            dma((16,)),
            dma((2,)),
            dma((2,)),
            dma((2, 4)),
            dma((2, 16)),
            dma((16,)),
            dma((16,)),
            dma((4,)),
            dma((4,)),
            dma((4,)),
            dma((2,)),
            dma((2, 16)),
            dma((5,)),
            dma((2,)),
            dma((2,)),
            dma((2,)),
        ],
        compiler_params=pltpu.CompilerParams(
            collective_id=0, has_side_effects=True, vmem_limit_bytes=67043328
        ),
        name="step",
    )(grad_out, scores.T, row_ids.T, proj_ids.T, values, proj_w.reshape(2, 4, 2, 128, 256))
    score_grads, value_grads, proj_grads = pl.pallas_call(
        hand_over, out_shape=shapes, in_specs=[vmem] * 3, out_specs=(vmem,) * 3, name="hand_over"
    )(*results)
    return score_grads.T, value_grads, proj_grads


def solution(mesh):
    return jax.shard_map(
        local,
        mesh=mesh,
        in_specs=(
            P(("mem", "dp"), None),
            P(("mem", "dp"), None),
            P(("mem", "dp"), None),
            P(("mem", "dp"), None),
            P("mem", None),
            P(None, None, "mem"),
        ),
        out_specs=(P(("mem", "dp"), None), P(("mem", "dp"), None), P(None, "dp", "mem")),
        check_vma=False,
    )
```
